32 devices in a mesh: occ: 4 (over y, core), vir: 8 (over z, x).
Axes of the slice: x: 2, y: 2, z: 4, core: 2. Of those that a mesh axis runs over, the one named last changes fastest.
Arguments:
- amplitudes: bfloat16 [32, 16, 128, 128], P(('occ', 'vir')), may hold values from -6 to 6
- amp_slots: int32 [32, 16], P(('occ', 'vir')), may hold values from 0 to 7, as said below
- integrals: bfloat16 [64, 48, 128, 128], P('vir', 'occ'), may hold values from -0.15625 to 0.15625
- int_columns: int32 [64, 48], replicated, may hold values from 0 to 63, as said below
- slot_tile: int32 [64], replicated, may hold values from 0 to 63, each once
Outputs:
- residual: bfloat16 [32, 16, 128, 128], P(('occ', 'vir'))
The draws below stay inside these ranges and needn't reach their ends.
Inputs may be any that keep to these rules, and one draw needn't show every extreme that they name: `amp_slots`: within each group of 2 consecutive slots of a row the values are distinct. `int_columns`: the 48 entries of a row are distinct.
All inputs are finite; a program needn't handle non-finite values.
Results may differ from the reference program's by a relative error of at most 0.012.
Values may be sent and summed in bfloat16 or wider, within the bound.
A program may use at most 192 MiB of HBM per device.

```python
import jax
import jax.numpy as jnp
from jax import lax

TILE_PAIR_COUNT = 128
OWNED_VIRT_TILES = 8
OWNED_ROW_TILES = 2
VIRTUAL_TILES = 64
ROW_SLOT_COUNT = 16
INTEGRAL_ROW_NNZ = 48
OCCUPIED_ROWS = 32


def draw_amp_slots(key, part):
    row_groupings = ROW_SLOT_COUNT // OWNED_ROW_TILES
    scores = jax.random.randint(key, (OCCUPIED_ROWS, row_groupings, OWNED_VIRT_TILES), 0, 1048576) * OWNED_VIRT_TILES + jnp.arange(OWNED_VIRT_TILES, dtype=jnp.int32)
    sorted_order = jnp.argsort(scores, axis=-1, stable=True).astype(jnp.int32)
    return sorted_order[:, :, :OWNED_ROW_TILES].reshape(OCCUPIED_ROWS, ROW_SLOT_COUNT)


def draw_int_columns(key, part):
    scores = jax.random.randint(key, (VIRTUAL_TILES, VIRTUAL_TILES), 0, 1048576) * VIRTUAL_TILES + jnp.arange(VIRTUAL_TILES, dtype=jnp.int32)
    sorted_order = jnp.argsort(scores, axis=-1, stable=True).astype(jnp.int32)
    return sorted_order[:, :INTEGRAL_ROW_NNZ]


def shard_levels(key, shape, cuts, least, high):
    factor_of = 1.0
    for axis_at, shards_of in cuts:
        steps = jax.random.uniform(jax.random.fold_in(jax.random.fold_in(key, 6), axis_at), (shards_of,), jnp.float32, least / len(cuts), high / len(cuts))
        factor_of = factor_of * jnp.repeat(jnp.exp(steps), shape[axis_at] // shards_of).reshape((-1,) + (1,) * (len(shape) - 1 - axis_at))
    return factor_of


def bell_draw(rng, extent, spread, limit, cuts=(), held_as=jnp.bfloat16):
    level = shard_levels(rng, extent, cuts, -0.22, 0.18) if cuts else 1.0
    array = jax.random.normal(rng, extent, jnp.float32) * spread * level
    return jnp.minimum(jnp.maximum(array, -limit), limit).astype(held_as)


def setup_inputs(seed: int = 0) -> dict:
    arg_keys = jax.random.split(jax.random.key(seed), 6)
    amplitudes = bell_draw(arg_keys[0], (OCCUPIED_ROWS, ROW_SLOT_COUNT, TILE_PAIR_COUNT, TILE_PAIR_COUNT), 1.0, 6.0, ((0, 32),))
    amp_slots = draw_amp_slots(jax.random.fold_in(arg_keys[5], 71), 0)
    integrals = bell_draw(arg_keys[2], (VIRTUAL_TILES, INTEGRAL_ROW_NNZ, TILE_PAIR_COUNT, TILE_PAIR_COUNT), (3 * ROW_SLOT_COUNT * TILE_PAIR_COUNT // 4) ** -0.5, 0.15625, ((0, 8), (1, 4)))
    int_columns = draw_int_columns(jax.random.fold_in(arg_keys[5], 71), 0)
    slot_tile = jax.random.permutation(arg_keys[4], VIRTUAL_TILES).astype(jnp.int32)
    return dict(amplitudes=amplitudes, amp_slots=amp_slots, integrals=integrals, int_columns=int_columns, slot_tile=slot_tile)


def reference(amplitudes, amp_slots, integrals, int_columns, slot_tile):
    owner_indices = ROW_SLOT_COUNT // OWNED_ROW_TILES
    start_offsets = (jnp.arange(ROW_SLOT_COUNT, dtype=jnp.int32) // OWNED_ROW_TILES) * OWNED_VIRT_TILES

    def one_row(pair):
        row_amps, row_slots = pair
        storage = (start_offsets + row_slots).astype(jnp.int32)
        tile_identifiers = slot_tile[storage]
        picked = integrals[storage].reshape(owner_indices, OWNED_ROW_TILES, INTEGRAL_ROW_NNZ, TILE_PAIR_COUNT, TILE_PAIR_COUNT)
        columns = int_columns[storage].reshape(owner_indices, OWNED_ROW_TILES, INTEGRAL_ROW_NNZ)
        grouped = row_amps.reshape(owner_indices, OWNED_ROW_TILES, TILE_PAIR_COUNT, TILE_PAIR_COUNT)

        def owner_term(triple):
            owner_amps, owner_ints, owner_cols = triple
            prods = jnp.einsum("kpq,kjqt->kjpt", owner_amps.astype(jnp.float32), owner_ints.astype(jnp.float32), precision=lax.Precision.HIGHEST)
            matches = (owner_cols[:, :, None] == tile_identifiers[None, None, :]).astype(jnp.float32)
            summed = jnp.einsum("kjs,kjpt->spt", matches, prods, precision=lax.Precision.HIGHEST)
            return summed.astype(jnp.bfloat16)

        terms = lax.map(owner_term, (grouped, picked, columns))
        return jnp.sum(terms.astype(jnp.float32), axis=0).astype(jnp.bfloat16)

    return lax.map(one_row, (amplitudes, amp_slots))
```

```python
import functools

import jax
import jax.numpy as jnp
from jax import lax
from jax.experimental import pallas as pl
from jax.experimental.pallas import tpu as pltpu
from jax.sharding import PartitionSpec as P

MESH = pl.DeviceIdType.MESH
CORES = 2
WIDTH = 16


def events_of(n_chunks, nz):
    events = []
    for c in range(n_chunks):
        events += [("gather", c, 0), ("compute", c, 0)]
        if c > 0:
            events.append(("finish", c - 1, 0))
        events += [("pass", c, i) for i in range(nz - 1)]
    return events + [("finish", n_chunks - 1, 0)]


def copies_of(dims, n_chunks):
    ny, nz, nx, _, owned, _ = dims
    nv = nz * nx
    per_chunk = (ny - 1) + ny + (nx - 1) * nz + (nz - 1)
    return n_chunks * per_chunk + (owned - 1) * (ny - 1) + 2 * (nv - 1)


def kernel(dims, n_chunks, own_slots, slot_tile, columns_t, amps_in, ints, out, *scratch):
    ny, nz, nx, slots, owned, share = dims
    tiles = owned * share
    nv, no = nz * nx, ny * CORES
    per_owner = slots // nv
    weights = scratch[:n_chunks]
    terms = scratch[n_chunks : 2 * n_chunks]
    from_x = scratch[2 * n_chunks : 3 * n_chunks]
    from_z = scratch[3 * n_chunks : 4 * n_chunks]
    (
        raw_ints, columns_of, tables, amp_raw, amps, tab_buf, tab_smem,
        near, send_sem, recv_sem, loc_sem,
    ) = scratch[4 * n_chunks :]

    occ, vir = lax.axis_index("occ"), lax.axis_index("vir")
    y, core = occ // CORES, lax.rem(occ, CORES)
    z, x = vir // nx, lax.rem(vir, nx)
    partner = y * CORES + (1 - core)

    def occ_at(step):
        return lax.rem(y + step, ny) * CORES + core

    def x_at(step):
        return lax.rem(x + step, nx)

    if nz == 4:
        z_to = [lax.rem(z + 2, 4), 3 - z, z + 1 - 2 * lax.rem(z, 2)]
        z_from = z_to
    else:
        z_to = [lax.rem(z + d, nz) for d in range(1, nz)]
        z_from = [lax.rem(z + nz - d, nz) for d in range(1, nz)]

    counts = {"remote": 0, "local": 0}
    sent = []

    def remote(src, dst, where):
        at = counts["remote"]
        counts["remote"] += 1
        copy = pltpu.make_async_remote_copy(
            src_ref=src, dst_ref=dst, send_sem=send_sem.at[at], recv_sem=recv_sem.at[at],
            device_id=where, device_id_type=MESH,
        )
        copy.start()
        sent.append(copy)
        return copy

    def local(src, dst):
        at = counts["local"]
        counts["local"] += 1
        copy = pltpu.make_async_copy(src, dst, loc_sem.at[at])
        copy.start()
        return copy

    def signal(sem, where):
        pl.semaphore_signal(sem, inc=1, device_id=where, device_id_type=MESH)

    def signal_plane(sem):
        for d in range(1, nx):
            signal(sem, {"occ": occ, "vir": z * nx + x_at(d)})

        @pl.when(z > 0)
        def _():
            signal(sem, {"occ": occ, "vir": vir - nx})

        @pl.when(z < nz - 1)
        def _():
            signal(sem, {"occ": occ, "vir": vir + nx})

    in_plane = (nx - 1) + (z + nz - 1) // nz + (2 * nz - 2 - z) // nz

    barrier = pltpu.get_barrier_semaphore()
    for d in range(1, ny):
        signal(barrier, {"occ": occ_at(d), "vir": vir})
    signal(barrier, {"occ": partner, "vir": vir})
    signal_plane(barrier)

    held = raw_ints.shape[0] // share

    def fetch(g):
        return local(
            ints.at[pl.ds(g * share, share)], raw_ints.at[pl.ds((g % held) * share, share)]
        )

    pieces_in = [fetch(g) for g in range(held)]
    amp_own = local(amps_in.at[vir], amp_raw.at[vir])

    def span(number, source):
        return weights[number].at[pl.ds(source * tiles, tiles)]

    for number in range(n_chunks):
        weights[number][no * tiles] = jnp.zeros((WIDTH, 128), jnp.bfloat16)

    def turn(slot, tile):
        turned = raw_ints[slot].T
        for number in range(n_chunks):
            weights[number][occ * tiles + tile] = turned[number * WIDTH : (number + 1) * WIDTH]

    across = {number: [[] for _ in range(ny - 1)] for number in range(n_chunks)}

    def start_lead(g):
        piece = weights[0].at[pl.ds(occ * tiles + g * share, share)]
        for d in range(1, ny):
            across[0][d - 1].append(remote(piece, piece, {"occ": occ_at(d), "vir": vir}))

    def start_across(number):
        for d in range(1, ny):
            across[number][d - 1].append(
                remote(span(number, occ), span(number, occ), {"occ": occ_at(d), "vir": vir})
            )

    for g in range(owned):
        pieces_in[g].wait()

        @pl.loop(0, share)
        def _(j, g=g):
            turn((g % held) * share + j, g * share + j)

        if g + held < owned:
            pieces_in.append(fetch(g + held))

        if g == 0:
            pl.semaphore_wait(barrier, ny + in_plane)
        start_lead(g)
        if 1 < g <= nz:
            pl.semaphore_wait(near.at[g - 2], in_plane)
        if 0 < g < nz:
            signal_plane(near.at[g - 1])

    for number in range(1, n_chunks):
        start_across(number)

    def send_amps(to):
        return remote(amps_in.at[to], amp_raw.at[vir], {"occ": occ, "vir": to})

    amp_copies = []
    for i in range(nz - 1):
        for d in range(nx):
            amp_copies.append((send_amps(z_to[i] * nx + x_at(d)), z_from[i] * nx + lax.rem(x + nx - d, nx)))
    for d in range(1, nx):
        amp_copies.append((send_amps(z * nx + x_at(d)), z * nx + lax.rem(x + nx - d, nx)))

    side = {}
    for number in range(n_chunks):
        side[number] = [
            remote(span(number, occ), span(number, occ), {"occ": partner, "vir": vir})
        ]

    columns_of[...] = columns_t[...].T
    rows = lax.broadcasted_iota(jnp.int32, (slots, share * no), 0)
    entry = lax.broadcasted_iota(jnp.int32, (slots, share * no), 1)
    place = (entry // share) * tiles + lax.rem(entry, share)
    wanted = jnp.zeros((slots, share * no), jnp.int32)
    for s in range(slots):
        wanted = jnp.where(rows == s, slot_tile[(s // per_owner) * owned + own_slots[0, s]], wanted)
    lanes = lax.broadcasted_iota(jnp.int32, (slots, 128), 1)
    for v in range(nv):
        mapped = jnp.zeros((slots, 128), jnp.int32)
        for k in range(per_owner):
            mine = own_slots[0, v * per_owner + k]
            reached = columns_of[pl.ds(v * owned + mine, 1), :]
            found = jnp.where(reached == wanted, place + mine * share, no * tiles)
            mapped = jnp.where(lanes == k, jnp.min(found, axis=1, keepdims=True), mapped)
        tables[v] = mapped

    tab_own = local(tables.at[vir], tab_buf.at[vir])
    tab_copies = []
    for d in range(1, nv):
        to = lax.rem(vir + d, nv)
        tab_copies.append(remote(tables.at[to], tab_buf.at[vir], {"occ": occ, "vir": to}))

    def turn_amps(v):
        for k in range(per_owner):
            amps[v, k * 128 : (k + 1) * 128, :] = amp_raw[v, k].T

    amp_own.wait()
    turn_amps(vir)
    for copy, source in amp_copies:
        copy.wait_recv()
        turn_amps(source)
    tab_own.wait()
    for copy in tab_copies:
        copy.wait_recv()
    local(tab_buf, tab_smem).wait()

    x_copies = {c: [[] for _ in range(nz)] for c in range(n_chunks)}
    z_copies = {c: [] for c in range(n_chunks)}

    def gather(c):
        for d in range(1, ny):
            for copy in across[c][d - 1]:
                copy.wait_recv()
            source = lax.rem(y - d + ny, ny) * CORES + core
            side[c].append(
                remote(span(c, source), span(c, source), {"occ": partner, "vir": vir})
            )

    def product(c, to_x, to_z):
        r = to_z * nx + to_x
        columns = []
        for k in range(per_owner):
            pieces = [weights[c][tab_smem[r, s, k]] for s in range(slots)]
            columns.append(jnp.concatenate(pieces, axis=0))
        left = jnp.concatenate(columns, axis=1)
        prod = jnp.dot(left, amps[r], preferred_element_type=jnp.float32)
        terms[c][to_x, to_z] = prod.astype(jnp.bfloat16).reshape(slots, WIDTH, 128)

    def compute(c):
        for copy in side[c]:
            copy.wait_recv()
        for i, to_z in enumerate(z_to + [z]):
            for d in range(1, nx):
                to_x = x_at(d)
                product(c, to_x, to_z)
                x_copies[c][i].append(
                    remote(
                        terms[c].at[to_x, to_z], from_x[c].at[d - 1, to_z],
                        {"occ": occ, "vir": z * nx + to_x},
                    )
                )
        for to_z in z_to + [z]:
            product(c, x, to_z)

    def x_total(c, i, to_z):
        for copy in x_copies[c][i]:
            copy.wait_recv()
        total = terms[c][x, to_z].astype(jnp.float32)
        for e in range(nx - 1):
            total += from_x[c][e, to_z].astype(jnp.float32)
        return total

    def pass_on(c, i):
        to_z = z_to[i]
        terms[c][x, to_z] = x_total(c, i, to_z).astype(jnp.bfloat16)
        z_copies[c].append(
            remote(terms[c].at[x, to_z], from_z[c].at[i], {"occ": occ, "vir": to_z * nx + x})
        )

    def finish(c):
        total = x_total(c, nz - 1, z)
        for e, copy in enumerate(z_copies[c]):
            copy.wait_recv()
            total += from_z[c][e].astype(jnp.float32)
        out[:, pl.ds(c * WIDTH, WIDTH), :] = total.astype(jnp.bfloat16)

    for what, c, i in events_of(n_chunks, nz):
        if what == "gather":
            gather(c)
        elif what == "compute":
            compute(c)
        elif what == "pass":
            pass_on(c, i)
        else:
            finish(c)
    for copy in sent:
        copy.wait_send()


def body(nx, amplitudes, amp_slots, integrals, int_columns, slot_tile):
    _, slots, tile, _ = amplitudes.shape
    nv, no = lax.axis_size("vir"), lax.axis_size("occ")
    ny, nz = no // CORES, nv // nx
    owned, share = integrals.shape[:2]
    tiles = owned * share
    per_owner = slots // nv
    n_chunks = tile // WIDTH
    dims = (ny, nz, nx, slots, owned, share)

    ints = integrals.reshape(tiles, tile, tile)
    amps = amplitudes.reshape(nv, per_owner, tile, tile)

    bf16 = jnp.bfloat16
    scratch = [pltpu.VMEM((no * tiles + 1, WIDTH, tile), bf16)] * n_chunks
    scratch += [pltpu.VMEM((nx, nz, slots, WIDTH, tile), bf16)] * n_chunks
    scratch += [pltpu.VMEM((nx - 1, nz, slots, WIDTH, tile), bf16)] * n_chunks
    scratch += [pltpu.VMEM((nz - 1, slots, WIDTH, tile), bf16)] * n_chunks
    n_copies = copies_of(dims, n_chunks)
    scratch += [
        pltpu.VMEM((min(4, owned) * share, tile, tile), bf16),
        pltpu.VMEM(int_columns.shape, jnp.int32),
        pltpu.VMEM((nv, slots, 128), jnp.int32),
        pltpu.VMEM((nv, per_owner, tile, tile), bf16),
        pltpu.VMEM((nv, per_owner * tile, tile), bf16),
        pltpu.VMEM((nv, slots, 128), jnp.int32),
        pltpu.SMEM((nv, slots, 128), jnp.int32),
        pltpu.SemaphoreType.REGULAR((nz - 1,)),
        pltpu.SemaphoreType.DMA((n_copies,)),
        pltpu.SemaphoreType.DMA((n_copies,)),
        pltpu.SemaphoreType.DMA((owned + 3,)),
    ]
    result = pl.pallas_call(
        functools.partial(kernel, dims, n_chunks),
        out_shape=jax.ShapeDtypeStruct((slots, tile, tile), bf16),
        in_specs=[
            pl.BlockSpec(memory_space=pltpu.SMEM),
            pl.BlockSpec(memory_space=pltpu.SMEM),
            pl.BlockSpec(memory_space=pltpu.VMEM),
            pl.BlockSpec(memory_space=pl.ANY),
            pl.BlockSpec(memory_space=pl.ANY),
        ],
        out_specs=pl.BlockSpec(memory_space=pltpu.VMEM),
        scratch_shapes=scratch,
        compiler_params=pltpu.CompilerParams(
            collective_id=0, has_side_effects=True, vmem_limit_bytes=66_000_000
        ),
    )(amp_slots, slot_tile, int_columns.T, amps, ints)
    return jnp.swapaxes(result, 1, 2)[None]


def solution(mesh):
    nv = mesh.shape["vir"]
    nx = nv // min(4, nv)
    in_specs = (
        P(("occ", "vir"), None, None, None),
        P(("occ", "vir"), None),
        P("vir", "occ", None, None),
        P(),
        P(),
    )
    out_specs = P(("occ", "vir"), None, None, None)
    return jax.shard_map(
        functools.partial(body, nx), mesh=mesh, in_specs=in_specs, out_specs=out_specs,
        check_vma=False,
    )
```

```python
import functools

import jax
import jax.numpy as jnp
from jax import lax
from jax.experimental import pallas as pl
from jax.experimental.pallas import tpu as pltpu
from jax.sharding import PartitionSpec as P

MESH = pl.DeviceIdType.MESH
CORES = 2
WIDTH = 16
HALF = 8


def events_of(n_full, n_chunks, nz):
    events = []
    last = nz - 2
    for c in range(n_chunks):
        order = [2, 0, 1] if c == 0 and nz == 4 else list(range(nz - 1))
        halves_after = c >= n_full - 1
        events.append(("gather", c, 0))
        if 0 < c < n_full:
            events.append(("pass", c - 1, 1 if c == 1 and nz == 4 else last))
        if c >= n_full and c > 1:
            events.append(("finish", c - 3, 0) if c > 2 else ("none", 0, 0))
        if c == n_full and c > 0:
            events.append(("pass", c - 1, order[0]))
        events.append(("compute", c, 0))
        if c == n_full and c > 0:
            events += [("pass", c - 1, i) for i in order[1:]]
        if c < n_full:
            if c > 1:
                events.append(("finish", c - 2, 0))
            if c < n_full - 1 or n_full == n_chunks:
                events += [("pass", c, i) for i in order[:-1]]
        elif c == n_chunks - 1:
            for late in range(n_full, n_chunks):
                events += [("pass", late, i) for i in range(nz - 1)]
    seen = set()
    unique = []
    for event in events:
        if event not in seen:
            seen.add(event)
            unique.append(event)
    for c in range(n_chunks):
        for i in range(nz - 1):
            if ("pass", c, i) not in seen:
                unique.append(("pass", c, i))
    for c in range(n_chunks):
        if ("finish", c, 0) not in seen:
            unique.append(("finish", c, 0))
    return [event for event in unique if event[0] != "none"]


def copies_of(dims, n_chunks):
    ny, nz, nx, _, owned, _ = dims
    nv = nz * nx
    per_chunk = (ny - 1) + ny + (nx - 1) * nz + (nz - 1)
    return n_chunks * per_chunk + (owned - 1) * (ny - 1) + 2 * (nv - 1)


def kernel(dims, halves, own_slots, slot_tile, columns_t, amps_in, ints, out, *scratch):
    ny, nz, nx, slots, owned, share = dims
    n_chunks, n_full = len(halves), halves.count(False)
    tiles = owned * share
    nv, no = nz * nx, ny * CORES
    per_owner = slots // nv
    weights = scratch[:n_chunks]
    terms = scratch[n_chunks : 2 * n_chunks]
    from_x = scratch[2 * n_chunks : 3 * n_chunks]
    from_z = scratch[3 * n_chunks : 4 * n_chunks]
    (
        raw_ints, columns_of, tables, amp_raw, amps, tab_buf, tab_smem, first_half,
        near, send_sem, recv_sem, loc_sem,
    ) = scratch[4 * n_chunks :]

    occ, vir = lax.axis_index("occ"), lax.axis_index("vir")
    y, core = occ // CORES, lax.rem(occ, CORES)
    z, x = vir // nx, lax.rem(vir, nx)
    partner = y * CORES + (1 - core)

    def occ_at(step):
        return lax.rem(y + step, ny) * CORES + core

    def x_at(step):
        return lax.rem(x + step, nx)

    if nz == 4:
        z_to = [lax.rem(z + 2, 4), 3 - z, z + 1 - 2 * lax.rem(z, 2)]
        z_from = z_to
        inner = (z == 1) | (z == 2)
        hops = [[(2, None)], [(1, inner), (3, jnp.logical_not(inner))], [(1, None)]]
        near_first = [3, 2, 0, 1]
    else:
        z_to = [lax.rem(z + d, nz) for d in range(1, nz)]
        z_from = [lax.rem(z + nz - d, nz) for d in range(1, nz)]
        hops = [[(nz - 1, None)]] * (nz - 1)
        near_first = [nz - 1] + list(range(nz - 1))
    z_all, z_all_from = z_to + [z], z_from + [z]
    hops.append([(0, None)])

    counts = {"remote": 0, "local": 0}
    sent = []

    def planned(src, dst, where):
        at = counts["remote"]
        counts["remote"] += 1
        copy = pltpu.make_async_remote_copy(
            src_ref=src, dst_ref=dst, send_sem=send_sem.at[at], recv_sem=recv_sem.at[at],
            device_id=where, device_id_type=MESH,
        )
        sent.append(copy)
        return copy

    def remote(src, dst, where):
        copy = planned(src, dst, where)
        copy.start()
        return copy

    def local(src, dst):
        at = counts["local"]
        counts["local"] += 1
        copy = pltpu.make_async_copy(src, dst, loc_sem.at[at])
        copy.start()
        return copy

    def signal(sem, where):
        pl.semaphore_signal(sem, inc=1, device_id=where, device_id_type=MESH)

    def signal_plane(sem):
        for d in range(1, nx):
            signal(sem, {"occ": occ, "vir": z * nx + x_at(d)})

        @pl.when(z > 0)
        def _():
            signal(sem, {"occ": occ, "vir": vir - nx})

        @pl.when(z < nz - 1)
        def _():
            signal(sem, {"occ": occ, "vir": vir + nx})

    in_plane = (nx - 1) + (z + nz - 1) // nz + (2 * nz - 2 - z) // nz

    barrier = pltpu.get_barrier_semaphore()
    for d in range(1, ny):
        signal(barrier, {"occ": occ_at(d), "vir": vir})
    signal(barrier, {"occ": partner, "vir": vir})
    signal_plane(barrier)

    held = raw_ints.shape[0] // share

    def fetch(g):
        return local(
            ints.at[pl.ds(g * share, share)], raw_ints.at[pl.ds((g % held) * share, share)]
        )

    pieces_in = [fetch(g) for g in range(held)]
    amp_own = local(amps_in.at[vir], amp_raw.at[vir])

    def span(number, source):
        held_tiles = tiles // 2 if halves[number] else tiles
        return weights[number].at[pl.ds(source * held_tiles, held_tiles)]

    for number in range(n_chunks):
        spare = no * tiles // 2 if halves[number] else no * tiles
        weights[number][spare] = jnp.zeros((WIDTH, 128), jnp.bfloat16)

    pair = 2 if n_full < n_chunks else 1

    def turn(slot, tile):
        tails = []
        for e in range(pair):
            turned = raw_ints[slot + e].T
            for number in range(n_full):
                weights[number][occ * tiles + tile + e] = turned[number * WIDTH : (number + 1) * WIDTH]
            if pair == 2:
                tails.append(turned[n_full * WIDTH : (n_full + 1) * WIDTH].astype(jnp.float32))
        for h in range(n_chunks - n_full):
            both = jnp.concatenate([tail[h * HALF : (h + 1) * HALF] for tail in tails], axis=0)
            weights[n_full + h][(occ * tiles + tile) // 2] = both.astype(jnp.bfloat16)

    across = {number: [[] for _ in range(ny - 1)] for number in range(n_chunks)}

    def start_lead(g):
        piece = weights[0].at[pl.ds(occ * tiles + g * share, share)]
        for d in range(1, ny):
            across[0][d - 1].append(remote(piece, piece, {"occ": occ_at(d), "vir": vir}))

    def start_across(number):
        for d in range(1, ny):
            across[number][d - 1].append(
                remote(span(number, occ), span(number, occ), {"occ": occ_at(d), "vir": vir})
            )

    amp_copies = {}
    for i in range(nz):
        for d in range(1 if i == nz - 1 else 0, nx):
            to = z_all[i] * nx + x_at(d)
            amp_copies[i, d] = planned(
                amps_in.at[to], amp_raw.at[vir], {"occ": occ, "vir": to}
            )

    def send_amps(level):
        for (i, d), copy in amp_copies.items():
            for hop, when in hops[i]:
                if hop + (1 if d else 0) == level:
                    if when is None:
                        copy.start()
                    else:
                        pl.when(when)(copy.start)

    columns_of[...] = columns_t[...].T
    rows = lax.broadcasted_iota(jnp.int32, (slots, share * no), 0)
    entry = lax.broadcasted_iota(jnp.int32, (slots, share * no), 1)
    place = (entry // share) * tiles + lax.rem(entry, share)
    wanted = jnp.zeros((slots, share * no), jnp.int32)
    for s in range(slots):
        wanted = jnp.where(rows == s, slot_tile[(s // per_owner) * owned + own_slots[0, s]], wanted)
    lanes = lax.broadcasted_iota(jnp.int32, (slots, 128), 1)

    def make_table(v):
        mapped = jnp.zeros((slots, 128), jnp.int32)
        for k in range(per_owner):
            mine = own_slots[0, v * per_owner + k]
            reached = columns_of[pl.ds(v * owned + mine, 1), :]
            found = jnp.where(reached == wanted, place + mine * share, no * tiles)
            mapped = jnp.where(lanes == k, jnp.min(found, axis=1, keepdims=True), mapped)
        tables[v] = mapped

    early = nv // 2
    for v in range(early):
        make_table(v)

    tab_copies = {}
    for g in range(owned):
        pieces_in[g].wait()

        @pl.loop(0, share // pair)
        def _(j, g=g):
            turn((g % held) * share + pair * j, g * share + pair * j)

        if g + held < owned:
            pieces_in.append(fetch(g + held))

        if g == 0:
            pl.semaphore_wait(barrier, ny + in_plane)
        start_lead(g)
        if 1 < g <= nz:
            pl.semaphore_wait(near.at[g - 2], in_plane)
        if 0 < g < nz:
            signal_plane(near.at[g - 1])
        if g != 1 and g <= nz:
            send_amps(max(g, 1))
        for v in range(early + g * (nv - early) // nz, early + (g + 1) * (nv - early) // nz):
            if v < nv:
                make_table(v)
        if g == nz:
            tab_own = local(tables.at[vir], tab_smem.at[vir])
            for i in near_first:
                for d in range(1 if i == nz - 1 else 0, nx):
                    to = z_all[i] * nx + x_at(d)
                    tab_copies[i, d] = remote(
                        tables.at[to], tab_buf.at[vir], {"occ": occ, "vir": to}
                    )

    for number in range(1, n_chunks):
        start_across(number)

    side = {}
    for number in range(n_chunks):
        side[number] = [
            remote(span(number, occ), span(number, occ), {"occ": partner, "vir": vir})
        ]

    def turn_amps(v):
        for k in range(per_owner):
            amps[v, k * 128 : (k + 1) * 128, :] = amp_raw[v, k].T

    amp_own.wait()
    tab_own.wait()
    turn_amps(vir)

    def prepare(i):
        started = []
        for d in range(1 if i == nz - 1 else 0, nx):
            source = z_all_from[i] * nx + lax.rem(x + nx - d, nx)
            tab_copies[i, d].wait_recv()
            started.append(local(tab_buf.at[source], tab_smem.at[source]))
        for d in range(1 if i == nz - 1 else 0, nx):
            source = z_all_from[i] * nx + lax.rem(x + nx - d, nx)
            amp_copies[i, d].wait_recv()
            turn_amps(source)
        for copy in started:
            copy.wait()

    if nz != 4:
        for i in near_first:
            prepare(i)

    x_copies = {c: [[] for _ in range(nz)] for c in range(n_chunks)}
    z_copies = {c: [] for c in range(n_chunks)}

    def gather(c):
        for d in range(1, ny):
            for copy in across[c][d - 1]:
                copy.wait_recv()
            source = lax.rem(y - d + ny, ny) * CORES + core
            side[c].append(
                remote(span(c, source), span(c, source), {"occ": partner, "vir": vir})
            )

    def product(c, to_x, to_z):
        r = to_z * nx + to_x
        if halves[c]:
            half_product(c, r, to_x, to_z)
            return
        columns = []
        for k in range(per_owner):
            pieces = [weights[c][tab_smem[r, s, k]] for s in range(slots)]
            columns.append(jnp.concatenate(pieces, axis=0))
        left = jnp.concatenate(columns, axis=1)
        prod = jnp.dot(left, amps[r], preferred_element_type=jnp.float32)
        terms[c][to_x, to_z] = prod.astype(jnp.bfloat16).reshape(slots, WIDTH, 128)

    def half_product(c, r, to_x, to_z):
        total = None
        for k in range(per_owner):
            at = [tab_smem[r, s, k] for s in range(slots)]
            left = jnp.concatenate(
                [weights[c][lax.shift_right_logical(a, 1)] for a in at], axis=0
            )
            prod = jnp.dot(
                left, amps[r, k * 128 : (k + 1) * 128, :], preferred_element_type=jnp.float32
            )
            picked = []
            for s, a in enumerate(at):
                low = prod[s * WIDTH : s * WIDTH + HALF]
                high = prod[s * WIDTH + HALF : (s + 1) * WIDTH]
                picked.append(jnp.where(lax.bitwise_and(a, 1) == 1, high, low))
            picked = jnp.concatenate(picked, axis=0)
            total = picked if total is None else total + picked
        terms[c][to_x, to_z] = total.reshape(slots // 2, WIDTH, 128).astype(jnp.bfloat16)

    def compute(c):
        for copy in side[c]:
            copy.wait_recv()
        for i in near_first if c == 0 else range(nz):
            to_z = z_all[i]
            if c == 0 and nz == 4:
                prepare(i)
            for d in range(1, nx):
                to_x = x_at(d)
                product(c, to_x, to_z)
                x_copies[c][i].append(
                    remote(
                        terms[c].at[to_x, to_z], from_x[c].at[d - 1, to_z],
                        {"occ": occ, "vir": z * nx + to_x},
                    )
                )
        for to_z in z_all:
            product(c, x, to_z)

    def x_total(c, i, to_z):
        for copy in x_copies[c][i]:
            copy.wait_recv()
        total = terms[c][x, to_z].astype(jnp.float32)
        for e in range(nx - 1):
            total += from_x[c][e, to_z].astype(jnp.float32)
        return total

    def pass_on(c, i):
        to_z = z_to[i]
        terms[c][x, to_z] = x_total(c, i, to_z).astype(jnp.bfloat16)
        z_copies[c].append(
            (i, remote(terms[c].at[x, to_z], from_z[c].at[i], {"occ": occ, "vir": to_z * nx + x}))
        )

    def finish(c):
        total = x_total(c, nz - 1, z)
        for e, copy in z_copies[c]:
            copy.wait_recv()
            total += from_z[c][e].astype(jnp.float32)
        if not halves[c]:
            out[:, pl.ds(c * WIDTH, WIDTH), :] = total.astype(jnp.bfloat16)
            return
        total = total.reshape(slots, HALF, 128)
        if c == n_full:
            first_half[...] = total
            return
        both = jnp.concatenate([first_half[...], total], axis=1)
        out[:, pl.ds(n_full * WIDTH, WIDTH), :] = both.astype(jnp.bfloat16)

    for what, c, i in events_of(n_full, n_chunks, nz):
        if what == "gather":
            gather(c)
        elif what == "compute":
            compute(c)
        elif what == "pass":
            pass_on(c, i)
        else:
            finish(c)
    for copy in sent:
        copy.wait_send()


def body(nx, amplitudes, amp_slots, integrals, int_columns, slot_tile):
    _, slots, tile, _ = amplitudes.shape
    nv, no = lax.axis_size("vir"), lax.axis_size("occ")
    ny, nz = no // CORES, nv // nx
    owned, share = integrals.shape[:2]
    tiles = owned * share
    per_owner = slots // nv
    n_chunks = tile // WIDTH
    halves = (False,) * n_chunks
    if share % 2 == 0 and slots % 2 == 0:
        halves = halves[1:] + (True, True)
        n_chunks += 1
    dims = (ny, nz, nx, slots, owned, share)

    ints = integrals.reshape(tiles, tile, tile)
    amps = amplitudes.reshape(nv, per_owner, tile, tile)

    bf16 = jnp.bfloat16
    held = [(no * tiles // 2, slots // 2) if half else (no * tiles, slots) for half in halves]
    scratch = [pltpu.VMEM((count + 1, WIDTH, tile), bf16) for count, _ in held]
    scratch += [pltpu.VMEM((nx, nz, part, WIDTH, tile), bf16) for _, part in held]
    scratch += [pltpu.VMEM((nx - 1, nz, part, WIDTH, tile), bf16) for _, part in held]
    scratch += [pltpu.VMEM((nz - 1, part, WIDTH, tile), bf16) for _, part in held]
    n_copies = copies_of(dims, n_chunks)
    scratch += [
        pltpu.VMEM((min(4, owned) * share, tile, tile), bf16),
        pltpu.VMEM(int_columns.shape, jnp.int32),
        pltpu.VMEM((nv, slots, 128), jnp.int32),
        pltpu.VMEM((nv, per_owner, tile, tile), bf16),
        pltpu.VMEM((nv, per_owner * tile, tile), bf16),
        pltpu.VMEM((nv, slots, 128), jnp.int32),
        pltpu.SMEM((nv, slots, 128), jnp.int32),
        pltpu.VMEM((slots, HALF, tile), jnp.float32),
        pltpu.SemaphoreType.REGULAR((nz - 1,)),
        pltpu.SemaphoreType.DMA((n_copies,)),
        pltpu.SemaphoreType.DMA((n_copies,)),
        pltpu.SemaphoreType.DMA((owned + 1 + nv,)),
    ]
    result = pl.pallas_call(
        functools.partial(kernel, dims, halves),
        out_shape=jax.ShapeDtypeStruct((slots, tile, tile), bf16),
        in_specs=[
            pl.BlockSpec(memory_space=pltpu.SMEM),
            pl.BlockSpec(memory_space=pltpu.SMEM),
            pl.BlockSpec(memory_space=pltpu.VMEM),
            pl.BlockSpec(memory_space=pl.ANY),
            pl.BlockSpec(memory_space=pl.ANY),
        ],
        out_specs=pl.BlockSpec(memory_space=pltpu.VMEM),
        scratch_shapes=scratch,
        compiler_params=pltpu.CompilerParams(
            collective_id=0, has_side_effects=True, vmem_limit_bytes=66_000_000
        ),
    )(amp_slots, slot_tile, int_columns.T, amps, ints)
    return jnp.swapaxes(result, 1, 2)[None]


def solution(mesh):
    nv = mesh.shape["vir"]
    nx = nv // min(4, nv)
    in_specs = (
        P(("occ", "vir"), None, None, None),
        P(("occ", "vir"), None),
        P("vir", "occ", None, None),
        P(),
        P(),
    )
    out_specs = P(("occ", "vir"), None, None, None)
    return jax.shard_map(
        functools.partial(body, nx), mesh=mesh, in_specs=in_specs, out_specs=out_specs,
        check_vma=False,
    )
```

```python
import functools

import jax
import jax.numpy as jnp
from jax import lax
from jax.experimental import pallas as pl
from jax.experimental.pallas import tpu as pltpu
from jax.sharding import PartitionSpec as P

MESH = pl.DeviceIdType.MESH
CORES = 2
WIDTH = 16
HALF = 8
SPLIT = 2


def events_of(n_full, n_chunks, nz):
    events = []
    steps = list(range(nz - 1))

    def order(c):
        return [2, 0, 1] if c == 0 and nz == 4 else steps

    def passes(c, at):
        return [("pass", c, i) for i in at]

    for c in range(n_chunks):
        events.append(("gather", c))
        before, after = [], []
        if 0 < c < n_full:
            before = passes(c - 1, order(c - 1)[-1:])
        elif c >= n_full and c > 0:
            early = 0 if c == n_full + 1 else 1
            before = passes(c - 1, order(c - 1)[:early])
            after = passes(c - 1, order(c - 1)[early:])
        if c < n_full - 1 or c == n_full - 1 == n_chunks - 1:
            after += passes(c, order(c)[:-1])
        if 1 < c < n_full:
            after = [("finish", c - 2)] + after
        elif c > n_full and c > 2:
            after.append(("finish", c - 3))
        events += before + [("compute", c)] + after
    listed = set(events)
    ends = [e for e in passes(n_chunks - 1, steps) if e not in listed]
    left = [("finish", c) for c in range(n_chunks) if ("finish", c) not in listed]
    return events + left[:-2] + ends + left[-2:]


def pieces_of(number, n_chunks, owned):
    if number == 0:
        return owned
    return 4 if number == n_chunks - 1 and owned % 4 == 0 else 1


def copies_of(dims, n_chunks):
    ny, nz, nx, _, owned, _ = dims
    nv = nz * nx
    per_chunk = 1 + (nx - 1) * nz + (nz - 1)
    pieces = sum(pieces_of(number, n_chunks, owned) for number in range(n_chunks))
    return n_chunks * per_chunk + 2 * pieces * (ny - 1) + 2 * (nv - 1)


def kernel(dims, halves, own_slots, slot_tile, columns_t, amps_in, ints, out, *scratch):
    ny, nz, nx, slots, owned, share = dims
    n_chunks, n_full = len(halves), halves.count(False)
    tiles = owned * share
    nv, no = nz * nx, ny * CORES
    per_owner = slots // nv
    weights = scratch[:n_chunks]
    terms = scratch[n_chunks : 2 * n_chunks]
    from_x = scratch[2 * n_chunks : 3 * n_chunks]
    from_z = scratch[3 * n_chunks : 4 * n_chunks]
    (
        raw_ints, columns_of, tables, amp_raw, amps, tab_buf, tab_smem, first_half,
        near, send_sem, recv_sem, loc_sem,
    ) = scratch[4 * n_chunks :]

    occ, vir = lax.axis_index("occ"), lax.axis_index("vir")
    y, core = occ // CORES, lax.rem(occ, CORES)
    z, x = vir // nx, lax.rem(vir, nx)
    partner = y * CORES + (1 - core)

    def occ_at(step):
        return lax.rem(y + step, ny) * CORES + core

    def x_at(step):
        return lax.rem(x + step, nx)

    if nz == 4:
        z_to = [lax.rem(z + 2, 4), 3 - z, z + 1 - 2 * lax.rem(z, 2)]
        z_from = z_to
        inner = (z == 1) | (z == 2)
        hops = [[(2, None)], [(1, inner), (3, jnp.logical_not(inner))], [(1, None)]]
        near_first = [3, 2, 0, 1]
    else:
        z_to = [lax.rem(z + d, nz) for d in range(1, nz)]
        z_from = [lax.rem(z + nz - d, nz) for d in range(1, nz)]
        hops = [[(nz - 1, None)]] * (nz - 1)
        near_first = [nz - 1] + list(range(nz - 1))
    z_all, z_all_from = z_to + [z], z_from + [z]
    hops.append([(0, None)])

    counts = {"remote": 0, "local": 0}
    sent = []

    def planned(src, dst, where):
        at = counts["remote"]
        counts["remote"] += 1
        copy = pltpu.make_async_remote_copy(
            src_ref=src, dst_ref=dst, send_sem=send_sem.at[at], recv_sem=recv_sem.at[at],
            device_id=where, device_id_type=MESH,
        )
        sent.append(copy)
        return copy

    def remote(src, dst, where):
        copy = planned(src, dst, where)
        copy.start()
        return copy

    def local(src, dst):
        at = counts["local"]
        counts["local"] += 1
        copy = pltpu.make_async_copy(src, dst, loc_sem.at[at])
        copy.start()
        return copy

    def signal(sem, where):
        pl.semaphore_signal(sem, inc=1, device_id=where, device_id_type=MESH)

    def signal_plane(sem):
        for d in range(1, nx):
            signal(sem, {"occ": occ, "vir": z * nx + x_at(d)})

        @pl.when(z > 0)
        def _():
            signal(sem, {"occ": occ, "vir": vir - nx})

        @pl.when(z < nz - 1)
        def _():
            signal(sem, {"occ": occ, "vir": vir + nx})

    in_plane = (nx - 1) + (z + nz - 1) // nz + (2 * nz - 2 - z) // nz

    barrier = pltpu.get_barrier_semaphore()
    for d in range(1, ny):
        signal(barrier, {"occ": occ_at(d), "vir": vir})
    signal(barrier, {"occ": partner, "vir": vir})
    signal_plane(barrier)

    held = raw_ints.shape[0] // share

    def fetch(g):
        return local(
            ints.at[pl.ds(g * share, share)], raw_ints.at[pl.ds((g % held) * share, share)]
        )

    pieces_in = [fetch(g) for g in range(held)]
    amp_own = local(amps_in.at[vir], amp_raw.at[vir])

    def span(number, source, piece=0, pieces=1):
        held_tiles = tiles // 2 if halves[number] else tiles
        count = held_tiles // pieces
        return weights[number].at[pl.ds(source * held_tiles + piece * count, count)]

    for number in range(n_chunks):
        spare = no * tiles // 2 if halves[number] else no * tiles
        weights[number][spare] = jnp.zeros((WIDTH, 128), jnp.bfloat16)

    pair = 2 if n_full < n_chunks else 1

    def turn(slot, tile):
        turned = [raw_ints[slot + e].T for e in range(pair)]
        for e in range(pair):
            for number in range(n_full):
                weights[number][occ * tiles + tile + e] = turned[e][number * WIDTH : (number + 1) * WIDTH]
        for number in range(n_full, n_chunks, 2):
            first = (n_full + (number - n_full) // 2) * WIDTH
            tails = [one[first : first + WIDTH].astype(jnp.float32) for one in turned]
            for h in range(2):
                both = jnp.concatenate([tail[h * HALF : (h + 1) * HALF] for tail in tails], axis=0)
                weights[number + h][(occ * tiles + tile) // 2] = both.astype(jnp.bfloat16)

    across = {number: [[] for _ in range(ny - 1)] for number in range(n_chunks)}

    def start_lead(g):
        piece = span(0, occ, g, owned)
        for d in range(1, ny):
            across[0][d - 1].append(remote(piece, piece, {"occ": occ_at(d), "vir": vir}))

    def start_across(number):
        pieces = pieces_of(number, n_chunks, owned)
        for p in range(pieces):
            piece = span(number, occ, p, pieces)
            for d in range(1, ny):
                across[number][d - 1].append(
                    remote(piece, piece, {"occ": occ_at(d), "vir": vir})
                )

    amp_copies = {}
    for i in range(nz):
        for d in range(1 if i == nz - 1 else 0, nx):
            to = z_all[i] * nx + x_at(d)
            amp_copies[i, d] = planned(
                amps_in.at[to], amp_raw.at[vir], {"occ": occ, "vir": to}
            )

    def send_amps(level):
        for (i, d), copy in amp_copies.items():
            for hop, when in hops[i]:
                if hop + (1 if d else 0) == level:
                    if when is None:
                        copy.start()
                    else:
                        pl.when(when)(copy.start)

    columns_of[...] = columns_t[...].T
    rows = lax.broadcasted_iota(jnp.int32, (slots, share * no), 0)
    entry = lax.broadcasted_iota(jnp.int32, (slots, share * no), 1)
    place = (entry // share) * tiles + lax.rem(entry, share)
    wanted = jnp.zeros((slots, share * no), jnp.int32)
    for s in range(slots):
        wanted = jnp.where(rows == s, slot_tile[(s // per_owner) * owned + own_slots[0, s]], wanted)
    lanes = lax.broadcasted_iota(jnp.int32, (slots, 128), 1)

    def make_table(v):
        mapped = jnp.zeros((slots, 128), jnp.int32)
        for k in range(per_owner):
            mine = own_slots[0, v * per_owner + k]
            reached = columns_of[pl.ds(v * owned + mine, 1), :]
            found = jnp.where(reached == wanted, place + mine * share, no * tiles)
            mapped = jnp.where(lanes == k, jnp.min(found, axis=1, keepdims=True), mapped)
        tables[v] = mapped

    early = nv // 4
    for v in range(early):
        make_table(v)

    tab_copies = {}
    for g in range(owned):
        pieces_in[g].wait()

        @pl.loop(0, share // pair)
        def _(j, g=g):
            turn((g % held) * share + pair * j, g * share + pair * j)

        if g + held < owned:
            pieces_in.append(fetch(g + held))

        if g == 0:
            pl.semaphore_wait(barrier, ny + in_plane)
        start_lead(g)
        if 1 < g <= nz:
            pl.semaphore_wait(near.at[g - 2], in_plane)
        if 0 < g < nz:
            signal_plane(near.at[g - 1])
        if g != 1 and g <= nz:
            send_amps(max(g, 1))
        for v in range(early + g * (nv - early) // nz, early + (g + 1) * (nv - early) // nz):
            if v < nv:
                make_table(v)
        if g == nz:
            tab_own = local(tables.at[vir], tab_smem.at[vir])
            for i in near_first:
                for d in range(1 if i == nz - 1 else 0, nx):
                    to = z_all[i] * nx + x_at(d)
                    tab_copies[i, d] = remote(
                        tables.at[to], tab_buf.at[vir], {"occ": occ, "vir": to}
                    )

    for number in range(1, n_chunks):
        start_across(number)

    side = {}
    for number in range(n_chunks):
        side[number] = [
            remote(span(number, occ), span(number, occ), {"occ": partner, "vir": vir})
        ]

    def turn_amps(v):
        for k in range(per_owner):
            amps[v, k * 128 : (k + 1) * 128, :] = amp_raw[v, k].T

    amp_own.wait()
    tab_own.wait()
    turn_amps(vir)

    def prepare(i):
        started = []
        for d in range(1 if i == nz - 1 else 0, nx):
            source = z_all_from[i] * nx + lax.rem(x + nx - d, nx)
            tab_copies[i, d].wait_recv()
            started.append(local(tab_buf.at[source], tab_smem.at[source]))
        for d in range(1 if i == nz - 1 else 0, nx):
            source = z_all_from[i] * nx + lax.rem(x + nx - d, nx)
            amp_copies[i, d].wait_recv()
            turn_amps(source)
        for copy in started:
            copy.wait()

    if nz != 4:
        for i in near_first:
            prepare(i)

    x_copies = {c: [[] for _ in range(nz)] for c in range(n_chunks)}
    z_copies = {c: [] for c in range(n_chunks)}

    def gather(c):
        for d in range(1, ny):
            source = lax.rem(y - d + ny, ny) * CORES + core
            for p, copy in enumerate(across[c][d - 1]):
                copy.wait_recv()
                piece = span(c, source, p, len(across[c][d - 1]))
                side[c].append(remote(piece, piece, {"occ": partner, "vir": vir}))

    def product(c, to_x, to_z):
        r = to_z * nx + to_x
        if halves[c]:
            half_product(c, r, to_x, to_z)
            return
        columns = []
        for k in range(per_owner):
            pieces = [weights[c][tab_smem[r, s, k]] for s in range(slots)]
            columns.append(jnp.concatenate(pieces, axis=0))
        left = jnp.concatenate(columns, axis=1)
        prod = jnp.dot(left, amps[r], preferred_element_type=jnp.float32)
        terms[c][to_x, to_z] = prod.astype(jnp.bfloat16).reshape(slots, WIDTH, 128)

    def half_product(c, r, to_x, to_z):
        total = None
        for k in range(per_owner):
            at = [tab_smem[r, s, k] for s in range(slots)]
            left = jnp.concatenate(
                [weights[c][lax.shift_right_logical(a, 1)] for a in at], axis=0
            )
            prod = jnp.dot(
                left, amps[r, k * 128 : (k + 1) * 128, :], preferred_element_type=jnp.float32
            )
            picked = []
            for s, a in enumerate(at):
                low = prod[s * WIDTH : s * WIDTH + HALF]
                high = prod[s * WIDTH + HALF : (s + 1) * WIDTH]
                picked.append(jnp.where(lax.bitwise_and(a, 1) == 1, high, low))
            picked = jnp.concatenate(picked, axis=0)
            total = picked if total is None else total + picked
        terms[c][to_x, to_z] = total.reshape(slots // 2, WIDTH, 128).astype(jnp.bfloat16)

    def compute(c):
        for copy in side[c]:
            copy.wait_recv()
        for i in near_first if c == 0 else range(nz):
            to_z = z_all[i]
            if c == 0 and nz == 4:
                prepare(i)
            for d in range(1, nx):
                to_x = x_at(d)
                product(c, to_x, to_z)
                x_copies[c][i].append(
                    remote(
                        terms[c].at[to_x, to_z], from_x[c].at[d - 1, to_z],
                        {"occ": occ, "vir": z * nx + to_x},
                    )
                )
        for to_z in z_all:
            product(c, x, to_z)

    def x_total(c, i, to_z):
        for copy in x_copies[c][i]:
            copy.wait_recv()
        total = terms[c][x, to_z].astype(jnp.float32)
        for e in range(nx - 1):
            total += from_x[c][e, to_z].astype(jnp.float32)
        return total

    def pass_on(c, i):
        to_z = z_to[i]
        terms[c][x, to_z] = x_total(c, i, to_z).astype(jnp.bfloat16)
        z_copies[c].append(
            (i, remote(terms[c].at[x, to_z], from_z[c].at[i], {"occ": occ, "vir": to_z * nx + x}))
        )

    def finish(c):
        total = x_total(c, nz - 1, z)
        for e, copy in z_copies[c]:
            copy.wait_recv()
            total += from_z[c][e].astype(jnp.float32)
        if not halves[c]:
            out[:, pl.ds(c * WIDTH, WIDTH), :] = total.astype(jnp.bfloat16)
            return
        total = total.reshape(slots, HALF, 128)
        if (c - n_full) % 2 == 0:
            first_half[...] = total
            return
        both = jnp.concatenate([first_half[...], total], axis=1)
        first = (n_full + (c - n_full) // 2) * WIDTH
        out[:, pl.ds(first, WIDTH), :] = both.astype(jnp.bfloat16)

    for what, c, *i in events_of(n_full, n_chunks, nz):
        if what == "gather":
            gather(c)
        elif what == "compute":
            compute(c)
        elif what == "pass":
            pass_on(c, *i)
        else:
            finish(c)
    for copy in sent:
        copy.wait_send()


def body(nx, amplitudes, amp_slots, integrals, int_columns, slot_tile):
    _, slots, tile, _ = amplitudes.shape
    nv, no = lax.axis_size("vir"), lax.axis_size("occ")
    ny, nz = no // CORES, nv // nx
    owned, share = integrals.shape[:2]
    tiles = owned * share
    per_owner = slots // nv
    n_chunks = tile // WIDTH
    halves = (False,) * n_chunks
    if share % 2 == 0 and slots % 2 == 0:
        halves = halves[SPLIT:] + (True, True) * SPLIT
        n_chunks += SPLIT
    dims = (ny, nz, nx, slots, owned, share)

    ints = integrals.reshape(tiles, tile, tile)
    amps = amplitudes.reshape(nv, per_owner, tile, tile)

    bf16 = jnp.bfloat16
    held = [(no * tiles // 2, slots // 2) if half else (no * tiles, slots) for half in halves]
    scratch = [pltpu.VMEM((count + 1, WIDTH, tile), bf16) for count, _ in held]
    scratch += [pltpu.VMEM((nx, nz, part, WIDTH, tile), bf16) for _, part in held]
    scratch += [pltpu.VMEM((nx - 1, nz, part, WIDTH, tile), bf16) for _, part in held]
    scratch += [pltpu.VMEM((nz - 1, part, WIDTH, tile), bf16) for _, part in held]
    n_copies = copies_of(dims, n_chunks)
    scratch += [
        pltpu.VMEM((min(4, owned) * share, tile, tile), bf16),
        pltpu.VMEM(int_columns.shape, jnp.int32),
        pltpu.VMEM((nv, slots, 128), jnp.int32),
        pltpu.VMEM((nv, per_owner, tile, tile), bf16),
        pltpu.VMEM((nv, per_owner * tile, tile), bf16),
        pltpu.VMEM((nv, slots, 128), jnp.int32),
        pltpu.SMEM((nv, slots, 128), jnp.int32),
        pltpu.VMEM((slots, HALF, tile), jnp.float32),
        pltpu.SemaphoreType.REGULAR((nz - 1,)),
        pltpu.SemaphoreType.DMA((n_copies,)),
        pltpu.SemaphoreType.DMA((n_copies,)),
        pltpu.SemaphoreType.DMA((owned + 1 + nv,)),
    ]
    result = pl.pallas_call(
        functools.partial(kernel, dims, halves),
        out_shape=jax.ShapeDtypeStruct((slots, tile, tile), bf16),
        in_specs=[
            pl.BlockSpec(memory_space=pltpu.SMEM),
            pl.BlockSpec(memory_space=pltpu.SMEM),
            pl.BlockSpec(memory_space=pltpu.VMEM),
            pl.BlockSpec(memory_space=pl.ANY),
            pl.BlockSpec(memory_space=pl.ANY),
        ],
        out_specs=pl.BlockSpec(memory_space=pltpu.VMEM),
        scratch_shapes=scratch,
        compiler_params=pltpu.CompilerParams(
            collective_id=0, has_side_effects=True, vmem_limit_bytes=66_000_000
        ),
    )(amp_slots, slot_tile, int_columns.T, amps, ints)
    return jnp.swapaxes(result, 1, 2)[None]


def solution(mesh):
    nv = mesh.shape["vir"]
    nx = nv // min(4, nv)
    in_specs = (
        P(("occ", "vir"), None, None, None),
        P(("occ", "vir"), None),
        P("vir", "occ", None, None),
        P(),
        P(),
    )
    out_specs = P(("occ", "vir"), None, None, None)
    return jax.shard_map(
        functools.partial(body, nx), mesh=mesh, in_specs=in_specs, out_specs=out_specs,
        check_vma=False,
    )
```

```python
import functools

import jax
import jax.numpy as jnp
from jax import lax
from jax.experimental import pallas as pl
from jax.experimental.pallas import tpu as pltpu
from jax.sharding import PartitionSpec as P

MESH = pl.DeviceIdType.MESH
CORES = 2
WIDTH = 16
HALF = 8
SPLIT = 2


def events_of(n_full, n_chunks, nz):
    events = []
    steps = list(range(nz - 1))

    def order(c):
        return [2, 0, 1] if c == 0 and nz == 4 else steps

    def passes(c, at):
        return [("pass", c, i) for i in at]

    for c in range(n_chunks):
        events.append(("gather", c))
        before, after = [], []
        if 0 < c < n_full:
            before = passes(c - 1, order(c - 1)[-1:])
        elif c >= n_full and c > 0:
            early = 0 if c == n_full + 1 else 1
            before = passes(c - 1, order(c - 1)[:early])
            after = passes(c - 1, order(c - 1)[early:])
        if c < n_full - 1 or c == n_full - 1 == n_chunks - 1:
            after += passes(c, order(c)[:-1])
        if 1 < c < n_full:
            after = [("finish", c - 2)] + after
        elif c > n_full and c > 2:
            after.append(("finish", c - 3))
        events += before + [("compute", c)] + after
    listed = set(events)
    ends = [e for e in passes(n_chunks - 1, steps) if e not in listed]
    left = [("finish", c) for c in range(n_chunks) if ("finish", c) not in listed]
    return events + left[:-2] + ends + left[-2:]


def pieces_of(number, n_chunks, owned):
    if number == 0:
        return owned
    return 4 if number == n_chunks - 1 and owned % 4 == 0 else 1


def copies_of(dims, n_chunks):
    ny, nz, nx, _, owned, _ = dims
    nv = nz * nx
    per_chunk = 1 + (nx - 1) * nz + (nz - 1)
    pieces = sum(pieces_of(number, n_chunks, owned) for number in range(n_chunks))
    return n_chunks * per_chunk + 2 * pieces * (ny - 1) + 2 * (nv - 1)


def kernel(dims, halves, slots_in, tiles_in, columns_in, amps_in, ints, out_at, *scratch):
    ny, nz, nx, slots, owned, share = dims
    n_chunks, n_full = len(halves), halves.count(False)
    tiles = owned * share
    nv, no = nz * nx, ny * CORES
    per_owner = slots // nv
    weights = scratch[:n_chunks]
    terms = scratch[n_chunks : 2 * n_chunks]
    from_x = scratch[2 * n_chunks : 3 * n_chunks]
    from_z = scratch[3 * n_chunks : 4 * n_chunks]
    (
        raw_ints, columns_of, tables, amp_raw, amps, tab_buf, tab_smem, first_half,
        own_slots, slot_tile, columns_t, out,
        near, send_sem, recv_sem, loc_sem,
    ) = scratch[4 * n_chunks :]

    occ, vir = lax.axis_index("occ"), lax.axis_index("vir")
    y, core = occ // CORES, lax.rem(occ, CORES)
    z, x = vir // nx, lax.rem(vir, nx)
    partner = y * CORES + (1 - core)

    def occ_at(step):
        return lax.rem(y + step, ny) * CORES + core

    def x_at(step):
        return lax.rem(x + step, nx)

    if nz == 4:
        z_to = [lax.rem(z + 2, 4), 3 - z, z + 1 - 2 * lax.rem(z, 2)]
        z_from = z_to
        inner = (z == 1) | (z == 2)
        hops = [[(2, None)], [(1, inner), (3, jnp.logical_not(inner))], [(1, None)]]
        near_first = [3, 2, 0, 1]
    else:
        z_to = [lax.rem(z + d, nz) for d in range(1, nz)]
        z_from = [lax.rem(z + nz - d, nz) for d in range(1, nz)]
        hops = [[(nz - 1, None)]] * (nz - 1)
        near_first = [nz - 1] + list(range(nz - 1))
    z_all, z_all_from = z_to + [z], z_from + [z]
    hops.append([(0, None)])

    counts = {"remote": 0, "local": 0}
    sent = []

    def planned(src, dst, where):
        at = counts["remote"]
        counts["remote"] += 1
        copy = pltpu.make_async_remote_copy(
            src_ref=src, dst_ref=dst, send_sem=send_sem.at[at], recv_sem=recv_sem.at[at],
            device_id=where, device_id_type=MESH,
        )
        sent.append(copy)
        return copy

    def remote(src, dst, where):
        copy = planned(src, dst, where)
        copy.start()
        return copy

    def local(src, dst):
        at = counts["local"]
        counts["local"] += 1
        copy = pltpu.make_async_copy(src, dst, loc_sem.at[at])
        copy.start()
        return copy

    def signal(sem, where):
        pl.semaphore_signal(sem, inc=1, device_id=where, device_id_type=MESH)

    def signal_plane(sem):
        for d in range(1, nx):
            signal(sem, {"occ": occ, "vir": z * nx + x_at(d)})

        @pl.when(z > 0)
        def _():
            signal(sem, {"occ": occ, "vir": vir - nx})

        @pl.when(z < nz - 1)
        def _():
            signal(sem, {"occ": occ, "vir": vir + nx})

    in_plane = (nx - 1) + (z + nz - 1) // nz + (2 * nz - 2 - z) // nz

    barrier = pltpu.get_barrier_semaphore()
    for d in range(1, ny):
        signal(barrier, {"occ": occ_at(d), "vir": vir})
    signal(barrier, {"occ": partner, "vir": vir})
    signal_plane(barrier)

    held = raw_ints.shape[0] // share

    def fetch(g):
        return local(
            ints.at[pl.ds(g * share, share)], raw_ints.at[pl.ds((g % held) * share, share)]
        )

    pieces_in = [fetch(g) for g in range(held)]
    amp_own = local(amps_in.at[vir], amp_raw.at[vir])
    lists_in = [
        local(slots_in, own_slots), local(tiles_in, slot_tile), local(columns_in, columns_t),
    ]

    def span(number, source, piece=0, pieces=1):
        held_tiles = tiles // 2 if halves[number] else tiles
        count = held_tiles // pieces
        return weights[number].at[pl.ds(source * held_tiles + piece * count, count)]

    for number in range(n_chunks):
        spare = no * tiles // 2 if halves[number] else no * tiles
        weights[number][spare] = jnp.zeros((WIDTH, 128), jnp.bfloat16)

    pair = 2 if n_full < n_chunks else 1

    def turn(slot, tile):
        turned = [raw_ints[slot + e].T for e in range(pair)]
        for e in range(pair):
            for number in range(n_full):
                weights[number][occ * tiles + tile + e] = turned[e][number * WIDTH : (number + 1) * WIDTH]
        for number in range(n_full, n_chunks, 2):
            first = (n_full + (number - n_full) // 2) * WIDTH
            tails = [one[first : first + WIDTH].astype(jnp.float32) for one in turned]
            for h in range(2):
                both = jnp.concatenate([tail[h * HALF : (h + 1) * HALF] for tail in tails], axis=0)
                weights[number + h][(occ * tiles + tile) // 2] = both.astype(jnp.bfloat16)

    across = {number: [[] for _ in range(ny - 1)] for number in range(n_chunks)}

    def start_lead(g):
        piece = span(0, occ, g, owned)
        for d in range(1, ny):
            across[0][d - 1].append(remote(piece, piece, {"occ": occ_at(d), "vir": vir}))

    def start_across(number):
        pieces = pieces_of(number, n_chunks, owned)
        for p in range(pieces):
            piece = span(number, occ, p, pieces)
            for d in range(1, ny):
                across[number][d - 1].append(
                    remote(piece, piece, {"occ": occ_at(d), "vir": vir})
                )

    amp_copies = {}
    for i in range(nz):
        for d in range(1 if i == nz - 1 else 0, nx):
            to = z_all[i] * nx + x_at(d)
            amp_copies[i, d] = planned(
                amps_in.at[to], amp_raw.at[vir], {"occ": occ, "vir": to}
            )

    def send_amps(level):
        for (i, d), copy in amp_copies.items():
            for hop, when in hops[i]:
                if hop + (1 if d else 0) == level:
                    if when is None:
                        copy.start()
                    else:
                        pl.when(when)(copy.start)

    for copy in lists_in:
        copy.wait()
    columns_of[...] = columns_t[...].T
    rows = lax.broadcasted_iota(jnp.int32, (slots, share * no), 0)
    entry = lax.broadcasted_iota(jnp.int32, (slots, share * no), 1)
    place = (entry // share) * tiles + lax.rem(entry, share)
    wanted = jnp.zeros((slots, share * no), jnp.int32)
    for s in range(slots):
        wanted = jnp.where(rows == s, slot_tile[(s // per_owner) * owned + own_slots[0, s]], wanted)
    lanes = lax.broadcasted_iota(jnp.int32, (slots, 128), 1)

    def make_table(v):
        mapped = jnp.zeros((slots, 128), jnp.int32)
        for k in range(per_owner):
            mine = own_slots[0, v * per_owner + k]
            reached = columns_of[pl.ds(v * owned + mine, 1), :]
            found = jnp.where(reached == wanted, place + mine * share, no * tiles)
            mapped = jnp.where(lanes == k, jnp.min(found, axis=1, keepdims=True), mapped)
        tables[v] = mapped

    early = nv // 4
    for v in range(early):
        make_table(v)

    relays = [1 + level * max(1, (owned - 2) // (nz - 1)) for level in range(nz)]
    tab_copies = {}
    for g in range(owned):
        pieces_in[g].wait()

        @pl.loop(0, share // pair)
        def _(j, g=g):
            turn((g % held) * share + pair * j, g * share + pair * j)

        if g + held < owned:
            pieces_in.append(fetch(g + held))

        if g == 0:
            pl.semaphore_wait(barrier, ny + in_plane)
        start_lead(g)
        if g == 0:
            send_amps(1)
        if g in relays:
            level = relays.index(g)
            if level > 0:
                pl.semaphore_wait(near.at[level - 1], in_plane)
                send_amps(level + 1)
            if level < nz - 1:
                signal_plane(near.at[level])
        for v in range(early + g * (nv - early) // owned, early + (g + 1) * (nv - early) // owned):
            make_table(v)
        if g == owned - 1:
            tab_own = local(tables.at[vir], tab_smem.at[vir])
            for i in near_first:
                for d in range(1 if i == nz - 1 else 0, nx):
                    to = z_all[i] * nx + x_at(d)
                    tab_copies[i, d] = remote(
                        tables.at[to], tab_buf.at[vir], {"occ": occ, "vir": to}
                    )

    for number in range(1, n_chunks):
        start_across(number)

    side = {}
    for number in range(n_chunks):
        side[number] = [
            remote(span(number, occ), span(number, occ), {"occ": partner, "vir": vir})
        ]

    def turn_amps(v):
        for k in range(per_owner):
            amps[v, k * 128 : (k + 1) * 128, :] = amp_raw[v, k].T

    amp_own.wait()
    tab_own.wait()
    turn_amps(vir)

    def prepare(i):
        started = []
        for d in range(1 if i == nz - 1 else 0, nx):
            source = z_all_from[i] * nx + lax.rem(x + nx - d, nx)
            tab_copies[i, d].wait_recv()
            started.append(local(tab_buf.at[source], tab_smem.at[source]))
        for d in range(1 if i == nz - 1 else 0, nx):
            source = z_all_from[i] * nx + lax.rem(x + nx - d, nx)
            amp_copies[i, d].wait_recv()
            turn_amps(source)
        for copy in started:
            copy.wait()

    if nz != 4:
        for i in near_first:
            prepare(i)

    x_copies = {c: [[] for _ in range(nz)] for c in range(n_chunks)}
    z_copies = {c: [] for c in range(n_chunks)}

    def gather(c):
        for d in range(1, ny):
            source = lax.rem(y - d + ny, ny) * CORES + core
            for p, copy in enumerate(across[c][d - 1]):
                copy.wait_recv()
                piece = span(c, source, p, len(across[c][d - 1]))
                side[c].append(remote(piece, piece, {"occ": partner, "vir": vir}))

    def product(c, to_x, to_z):
        r = to_z * nx + to_x
        if halves[c]:
            half_product(c, r, to_x, to_z)
            return
        columns = []
        for k in range(per_owner):
            pieces = [weights[c][tab_smem[r, s, k]] for s in range(slots)]
            columns.append(jnp.concatenate(pieces, axis=0))
        left = jnp.concatenate(columns, axis=1)
        prod = jnp.dot(left, amps[r], preferred_element_type=jnp.float32)
        terms[c][to_x, to_z] = prod.astype(jnp.bfloat16).reshape(slots, WIDTH, 128)

    def half_product(c, r, to_x, to_z):
        total = None
        for k in range(per_owner):
            at = [tab_smem[r, s, k] for s in range(slots)]
            left = jnp.concatenate(
                [weights[c][lax.shift_right_logical(a, 1)] for a in at], axis=0
            )
            prod = jnp.dot(
                left, amps[r, k * 128 : (k + 1) * 128, :], preferred_element_type=jnp.float32
            )
            picked = []
            for s, a in enumerate(at):
                low = prod[s * WIDTH : s * WIDTH + HALF]
                high = prod[s * WIDTH + HALF : (s + 1) * WIDTH]
                picked.append(jnp.where(lax.bitwise_and(a, 1) == 1, high, low))
            picked = jnp.concatenate(picked, axis=0)
            total = picked if total is None else total + picked
        terms[c][to_x, to_z] = total.reshape(slots // 2, WIDTH, 128).astype(jnp.bfloat16)

    def compute(c):
        for copy in side[c]:
            copy.wait_recv()
        for i in near_first if c == 0 else range(nz):
            to_z = z_all[i]
            if c == 0 and nz == 4:
                prepare(i)
            for d in range(1, nx):
                to_x = x_at(d)
                product(c, to_x, to_z)
                x_copies[c][i].append(
                    remote(
                        terms[c].at[to_x, to_z], from_x[c].at[d - 1, to_z],
                        {"occ": occ, "vir": z * nx + to_x},
                    )
                )
        for to_z in z_all:
            product(c, x, to_z)

    def x_total(c, i, to_z):
        for copy in x_copies[c][i]:
            copy.wait_recv()
        total = terms[c][x, to_z].astype(jnp.float32)
        for e in range(nx - 1):
            total += from_x[c][e, to_z].astype(jnp.float32)
        return total

    def pass_on(c, i):
        to_z = z_to[i]
        terms[c][x, to_z] = x_total(c, i, to_z).astype(jnp.bfloat16)
        z_copies[c].append(
            (i, remote(terms[c].at[x, to_z], from_z[c].at[i], {"occ": occ, "vir": to_z * nx + x}))
        )

    outgoing = []

    def hand_over(first, values):
        at = pl.ds(first, WIDTH)
        out[:, at, :] = values.astype(jnp.bfloat16)
        outgoing.append(local(out.at[:, at, :], out_at.at[:, at, :]))

    def finish(c):
        total = x_total(c, nz - 1, z)
        for e, copy in z_copies[c]:
            copy.wait_recv()
            total += from_z[c][e].astype(jnp.float32)
        if not halves[c]:
            hand_over(c * WIDTH, total)
            return
        total = total.reshape(slots, HALF, 128)
        if (c - n_full) % 2 == 0:
            first_half[...] = total
            return
        both = jnp.concatenate([first_half[...], total], axis=1)
        first = (n_full + (c - n_full) // 2) * WIDTH
        hand_over(first, both)

    for what, c, *i in events_of(n_full, n_chunks, nz):
        if what == "gather":
            gather(c)
        elif what == "compute":
            compute(c)
        elif what == "pass":
            pass_on(c, *i)
        else:
            finish(c)
    for copy in outgoing:
        copy.wait()
    for copy in sent:
        copy.wait_send()


def body(nx, amplitudes, amp_slots, integrals, int_columns, slot_tile):
    _, slots, tile, _ = amplitudes.shape
    nv, no = lax.axis_size("vir"), lax.axis_size("occ")
    ny, nz = no // CORES, nv // nx
    owned, share = integrals.shape[:2]
    tiles = owned * share
    per_owner = slots // nv
    n_chunks = tile // WIDTH
    halves = (False,) * n_chunks
    if share % 2 == 0 and slots % 2 == 0:
        halves = halves[SPLIT:] + (True, True) * SPLIT
        n_chunks += SPLIT
    dims = (ny, nz, nx, slots, owned, share)

    ints = integrals.reshape(tiles, tile, tile)
    amps = amplitudes.reshape(nv, per_owner, tile, tile)

    bf16 = jnp.bfloat16
    held = [(no * tiles // 2, slots // 2) if half else (no * tiles, slots) for half in halves]
    scratch = [pltpu.VMEM((count + 1, WIDTH, tile), bf16) for count, _ in held]
    scratch += [pltpu.VMEM((nx, nz, part, WIDTH, tile), bf16) for _, part in held]
    scratch += [pltpu.VMEM((nx - 1, nz, part, WIDTH, tile), bf16) for _, part in held]
    scratch += [pltpu.VMEM((nz - 1, part, WIDTH, tile), bf16) for _, part in held]
    n_copies = copies_of(dims, n_chunks)
    scratch += [
        pltpu.VMEM((min(4, owned) * share, tile, tile), bf16),
        pltpu.VMEM(int_columns.shape, jnp.int32),
        pltpu.VMEM((nv, slots, 128), jnp.int32),
        pltpu.VMEM((nv, per_owner, tile, tile), bf16),
        pltpu.VMEM((nv, per_owner * tile, tile), bf16),
        pltpu.VMEM((nv, slots, 128), jnp.int32),
        pltpu.SMEM((nv, slots, 128), jnp.int32),
        pltpu.VMEM((slots, HALF, tile), jnp.float32),
        pltpu.SMEM(amp_slots.shape, jnp.int32),
        pltpu.SMEM(slot_tile.shape, jnp.int32),
        pltpu.VMEM(int_columns.shape[::-1], jnp.int32),
        pltpu.VMEM((slots, tile, tile), bf16),
        pltpu.SemaphoreType.REGULAR((nz - 1,)),
        pltpu.SemaphoreType.DMA((n_copies,)),
        pltpu.SemaphoreType.DMA((n_copies,)),
        pltpu.SemaphoreType.DMA((owned + 4 + nv + tile // WIDTH,)),
    ]
    result = pl.pallas_call(
        functools.partial(kernel, dims, halves),
        out_shape=jax.ShapeDtypeStruct((slots, tile, tile), bf16),
        in_specs=[
            pl.BlockSpec(memory_space=pl.ANY),
            pl.BlockSpec(memory_space=pl.ANY),
            pl.BlockSpec(memory_space=pl.ANY),
            pl.BlockSpec(memory_space=pl.ANY),
            pl.BlockSpec(memory_space=pl.ANY),
        ],
        out_specs=pl.BlockSpec(memory_space=pl.ANY),
        scratch_shapes=scratch,
        compiler_params=pltpu.CompilerParams(
            collective_id=0, has_side_effects=True, vmem_limit_bytes=66_000_000
        ),
    )(amp_slots, slot_tile, int_columns.T, amps, ints)
    return jnp.swapaxes(result, 1, 2)[None]


def solution(mesh):
    nv = mesh.shape["vir"]
    nx = nv // min(4, nv)
    in_specs = (
        P(("occ", "vir"), None, None, None),
        P(("occ", "vir"), None),
        P("vir", "occ", None, None),
        P(),
        P(),
    )
    out_specs = P(("occ", "vir"), None, None, None)
    return jax.shard_map(
        functools.partial(body, nx), mesh=mesh, in_specs=in_specs, out_specs=out_specs,
        check_vma=False,
    )
```

```python
import functools

import jax
import jax.numpy as jnp
from jax import lax
from jax.experimental import pallas as pl
from jax.experimental.pallas import tpu as pltpu
from jax.sharding import PartitionSpec as P

MESH = pl.DeviceIdType.MESH
CORES = 2
WIDTH = 16
HALF = 8
SPLIT = 2


def events_of(n_full, n_chunks, nz):
    events = []
    steps = list(range(nz - 1))

    def order(c):
        return [2, 0, 1] if c == 0 and nz == 4 else steps

    def passes(c, at):
        return [("pass", c, i) for i in at]

    for c in range(n_chunks):
        events.append(("gather", c))
        before, after = [], []
        if 0 < c < n_full:
            before = passes(c - 1, order(c - 1)[-1:])
        elif c >= n_full and c > 0:
            early = 0 if c == n_full + 1 else 1
            before = passes(c - 1, order(c - 1)[:early])
            after = passes(c - 1, order(c - 1)[early:])
        if c < n_full - 1 or c == n_full - 1 == n_chunks - 1:
            after += passes(c, order(c)[:-1])
        if 1 < c < n_full:
            after = [("finish", c - 2)] + after
        elif c > n_full and c > 2:
            after.append(("finish", c - 3))
        compute = [("compute", c), ("own", c)]
        if c == n_chunks - 1:
            after[2:2] = compute[1:]
            compute = compute[:1]
        events += before + compute + after
    listed = set(events)
    ends = [e for e in passes(n_chunks - 1, steps) if e not in listed]
    left = [("finish", c) for c in range(n_chunks) if ("finish", c) not in listed]
    return events + left[:-2] + ends + left[-2:]


def pieces_of(number, n_chunks, owned):
    if number == 0:
        return owned
    return 1


def copies_of(dims, n_chunks):
    ny, nz, nx, _, owned, _ = dims
    nv = nz * nx
    per_chunk = 1 + (nx - 1) * nz + (nz - 1)
    pieces = sum(pieces_of(number, n_chunks, owned) for number in range(n_chunks))
    return n_chunks * per_chunk + 2 * pieces * (ny - 1) + 2 * (nv - 1)


def kernel(dims, halves, slots_in, tiles_in, columns_in, amps_in, ints, out_at, *scratch):
    ny, nz, nx, slots, owned, share = dims
    n_chunks, n_full = len(halves), halves.count(False)
    tiles = owned * share
    nv, no = nz * nx, ny * CORES
    per_owner = slots // nv
    weights = scratch[:n_chunks]
    terms = scratch[n_chunks : 2 * n_chunks]
    from_x = scratch[2 * n_chunks : 3 * n_chunks]
    from_z = scratch[3 * n_chunks : 4 * n_chunks]
    (
        raw_ints, columns_of, tables, amp_raw, amps, tab_buf, tab_smem, first_half,
        own_slots, slot_tile, columns_t, out,
        near, send_sem, recv_sem, loc_sem,
    ) = scratch[4 * n_chunks :]

    occ, vir = lax.axis_index("occ"), lax.axis_index("vir")
    y, core = occ // CORES, lax.rem(occ, CORES)
    z, x = vir // nx, lax.rem(vir, nx)
    partner = y * CORES + (1 - core)

    def occ_at(step):
        return lax.rem(y + step, ny) * CORES + core

    def x_at(step):
        return lax.rem(x + step, nx)

    if nz == 4:
        z_to = [lax.rem(z + 2, 4), 3 - z, z + 1 - 2 * lax.rem(z, 2)]
        z_from = z_to
        inner = (z == 1) | (z == 2)
        hops = [[(2, None)], [(1, inner), (3, jnp.logical_not(inner))], [(1, None)]]
        near_first = [3, 2, 0, 1]
    else:
        z_to = [lax.rem(z + d, nz) for d in range(1, nz)]
        z_from = [lax.rem(z + nz - d, nz) for d in range(1, nz)]
        hops = [[(nz - 1, None)]] * (nz - 1)
        near_first = [nz - 1] + list(range(nz - 1))
    z_all, z_all_from = z_to + [z], z_from + [z]
    hops.append([(0, None)])

    counts = {"remote": 0, "local": 0}
    sent = []

    def planned(src, dst, where):
        at = counts["remote"]
        counts["remote"] += 1
        copy = pltpu.make_async_remote_copy(
            src_ref=src, dst_ref=dst, send_sem=send_sem.at[at], recv_sem=recv_sem.at[at],
            device_id=where, device_id_type=MESH,
        )
        sent.append(copy)
        return copy

    def remote(src, dst, where):
        copy = planned(src, dst, where)
        copy.start()
        return copy

    def local(src, dst):
        at = counts["local"]
        counts["local"] += 1
        copy = pltpu.make_async_copy(src, dst, loc_sem.at[at])
        copy.start()
        return copy

    def signal(sem, where):
        pl.semaphore_signal(sem, inc=1, device_id=where, device_id_type=MESH)

    def signal_plane(sem):
        for d in range(1, nx):
            signal(sem, {"occ": occ, "vir": z * nx + x_at(d)})

        @pl.when(z > 0)
        def _():
            signal(sem, {"occ": occ, "vir": vir - nx})

        @pl.when(z < nz - 1)
        def _():
            signal(sem, {"occ": occ, "vir": vir + nx})

    in_plane = (nx - 1) + (z + nz - 1) // nz + (2 * nz - 2 - z) // nz

    barrier = pltpu.get_barrier_semaphore()
    for d in range(1, ny):
        signal(barrier, {"occ": occ_at(d), "vir": vir})
    signal(barrier, {"occ": partner, "vir": vir})
    signal_plane(barrier)

    held = raw_ints.shape[0] // share

    def fetch(g):
        return local(
            ints.at[pl.ds(g * share, share)], raw_ints.at[pl.ds((g % held) * share, share)]
        )

    pieces_in = [fetch(g) for g in range(held)]
    amp_own = local(amps_in.at[vir], amp_raw.at[vir])
    lists_in = [
        local(slots_in, own_slots), local(tiles_in, slot_tile), local(columns_in, columns_t),
    ]

    def span(number, source, piece=0, pieces=1):
        held_tiles = tiles // 2 if halves[number] else tiles
        count = held_tiles // pieces
        return weights[number].at[pl.ds(source * held_tiles + piece * count, count)]

    for number in range(n_chunks):
        spare = no * tiles // 2 if halves[number] else no * tiles
        weights[number][spare] = jnp.zeros((WIDTH, 128), jnp.bfloat16)

    pair = 2 if n_full < n_chunks else 1

    def turn(slot, tile):
        turned = [raw_ints[slot + e].T for e in range(pair)]
        for e in range(pair):
            for number in range(n_full):
                weights[number][occ * tiles + tile + e] = turned[e][number * WIDTH : (number + 1) * WIDTH]
        for number in range(n_full, n_chunks, 2):
            first = (n_full + (number - n_full) // 2) * WIDTH
            tails = [one[first : first + WIDTH].astype(jnp.float32) for one in turned]
            for h in range(2):
                both = jnp.concatenate([tail[h * HALF : (h + 1) * HALF] for tail in tails], axis=0)
                weights[number + h][(occ * tiles + tile) // 2] = both.astype(jnp.bfloat16)

    across = {number: [[] for _ in range(ny - 1)] for number in range(n_chunks)}

    def start_lead(g):
        piece = span(0, occ, g, owned)
        for d in range(1, ny):
            across[0][d - 1].append(remote(piece, piece, {"occ": occ_at(d), "vir": vir}))

    def start_across(number):
        pieces = pieces_of(number, n_chunks, owned)
        for p in range(pieces):
            piece = span(number, occ, p, pieces)
            for d in range(1, ny):
                across[number][d - 1].append(
                    remote(piece, piece, {"occ": occ_at(d), "vir": vir})
                )

    amp_copies = {}
    for i in range(nz):
        for d in range(1 if i == nz - 1 else 0, nx):
            to = z_all[i] * nx + x_at(d)
            amp_copies[i, d] = planned(
                amps_in.at[to], amp_raw.at[vir], {"occ": occ, "vir": to}
            )

    def send_amps(level):
        for (i, d), copy in amp_copies.items():
            for hop, when in hops[i]:
                if hop + (1 if d else 0) == level:
                    if when is None:
                        copy.start()
                    else:
                        pl.when(when)(copy.start)

    for copy in lists_in:
        copy.wait()
    columns_of[...] = columns_t[...].T
    rows = lax.broadcasted_iota(jnp.int32, (slots, share * no), 0)
    entry = lax.broadcasted_iota(jnp.int32, (slots, share * no), 1)
    place = (entry // share) * tiles + lax.rem(entry, share)
    wanted = jnp.zeros((slots, share * no), jnp.int32)
    for s in range(slots):
        wanted = jnp.where(rows == s, slot_tile[(s // per_owner) * owned + own_slots[0, s]], wanted)
    lanes = lax.broadcasted_iota(jnp.int32, (slots, 128), 1)

    def make_table(v):
        mapped = jnp.zeros((slots, 128), jnp.int32)
        for k in range(per_owner):
            mine = own_slots[0, v * per_owner + k]
            reached = columns_of[pl.ds(v * owned + mine, 1), :]
            found = jnp.where(reached == wanted, place + mine * share, no * tiles)
            mapped = jnp.where(lanes == k, jnp.min(found, axis=1, keepdims=True), mapped)
        tables[v] = mapped

    early = nv // 4
    for v in range(early):
        make_table(v)

    relays = [1 + level * max(1, (owned - 2) // (nz - 1)) for level in range(nz)]
    tab_copies = {}
    for g in range(owned):
        pieces_in[g].wait()

        @pl.loop(0, share // pair)
        def _(j, g=g):
            turn((g % held) * share + pair * j, g * share + pair * j)

        if g + held < owned:
            pieces_in.append(fetch(g + held))

        if g == 0:
            pl.semaphore_wait(barrier, ny + in_plane)
        start_lead(g)
        if g == 0:
            send_amps(1)
        if g in relays:
            level = relays.index(g)
            if level > 0:
                pl.semaphore_wait(near.at[level - 1], in_plane)
                send_amps(level + 1)
            if level < nz - 1:
                signal_plane(near.at[level])
        for v in range(early + g * (nv - early) // owned, early + (g + 1) * (nv - early) // owned):
            make_table(v)
        if g == owned - 1:
            tab_own = local(tables.at[vir], tab_smem.at[vir])
            for i in near_first:
                for d in range(1 if i == nz - 1 else 0, nx):
                    to = z_all[i] * nx + x_at(d)
                    tab_copies[i, d] = remote(
                        tables.at[to], tab_buf.at[vir], {"occ": occ, "vir": to}
                    )

    for number in range(1, n_chunks):
        start_across(number)

    side = {}
    for number in range(n_chunks):
        side[number] = [
            remote(span(number, occ), span(number, occ), {"occ": partner, "vir": vir})
        ]

    def turn_amps(v):
        for k in range(per_owner):
            amps[v, k * 128 : (k + 1) * 128, :] = amp_raw[v, k].T

    amp_own.wait()
    tab_own.wait()
    turn_amps(vir)

    def prepare(i):
        started = []
        for d in range(1 if i == nz - 1 else 0, nx):
            source = z_all_from[i] * nx + lax.rem(x + nx - d, nx)
            tab_copies[i, d].wait_recv()
            started.append(local(tab_buf.at[source], tab_smem.at[source]))
        for d in range(1 if i == nz - 1 else 0, nx):
            source = z_all_from[i] * nx + lax.rem(x + nx - d, nx)
            amp_copies[i, d].wait_recv()
            turn_amps(source)
        for copy in started:
            copy.wait()

    if nz != 4:
        for i in near_first:
            prepare(i)

    x_copies = {c: [[] for _ in range(nz)] for c in range(n_chunks)}
    z_copies = {c: [] for c in range(n_chunks)}

    def gather(c):
        for d in range(1, ny):
            source = lax.rem(y - d + ny, ny) * CORES + core
            for p, copy in enumerate(across[c][d - 1]):
                copy.wait_recv()
                piece = span(c, source, p, len(across[c][d - 1]))
                side[c].append(remote(piece, piece, {"occ": partner, "vir": vir}))

    def product(c, to_x, to_z):
        r = to_z * nx + to_x
        if halves[c]:
            half_product(c, r, to_x, to_z)
            return
        columns = []
        for k in range(per_owner):
            pieces = [weights[c][tab_smem[r, s, k]] for s in range(slots)]
            columns.append(jnp.concatenate(pieces, axis=0))
        left = jnp.concatenate(columns, axis=1)
        prod = jnp.dot(left, amps[r], preferred_element_type=jnp.float32)
        terms[c][to_x, to_z] = prod.astype(jnp.bfloat16).reshape(slots, WIDTH, 128)

    def half_product(c, r, to_x, to_z):
        total = None
        for k in range(per_owner):
            at = [tab_smem[r, s, k] for s in range(slots)]
            left = jnp.concatenate(
                [weights[c][lax.shift_right_logical(a, 1)] for a in at], axis=0
            )
            prod = jnp.dot(
                left, amps[r, k * 128 : (k + 1) * 128, :], preferred_element_type=jnp.float32
            )
            picked = []
            for s, a in enumerate(at):
                low = prod[s * WIDTH : s * WIDTH + HALF]
                high = prod[s * WIDTH + HALF : (s + 1) * WIDTH]
                picked.append(jnp.where(lax.bitwise_and(a, 1) == 1, high, low))
            picked = jnp.concatenate(picked, axis=0)
            total = picked if total is None else total + picked
        terms[c][to_x, to_z] = total.reshape(slots // 2, WIDTH, 128).astype(jnp.bfloat16)

    def compute(c):
        for copy in side[c]:
            copy.wait_recv()
        for i in near_first if c == 0 else range(nz):
            to_z = z_all[i]
            if c == 0 and nz == 4:
                prepare(i)
            for d in range(1, nx):
                to_x = x_at(d)
                product(c, to_x, to_z)
                x_copies[c][i].append(
                    remote(
                        terms[c].at[to_x, to_z], from_x[c].at[d - 1, to_z],
                        {"occ": occ, "vir": z * nx + to_x},
                    )
                )

    def compute_own(c):
        for to_z in z_all:
            product(c, x, to_z)

    def x_total(c, i, to_z):
        for copy in x_copies[c][i]:
            copy.wait_recv()
        total = terms[c][x, to_z].astype(jnp.float32)
        for e in range(nx - 1):
            total += from_x[c][e, to_z].astype(jnp.float32)
        return total

    def pass_on(c, i):
        to_z = z_to[i]
        terms[c][x, to_z] = x_total(c, i, to_z).astype(jnp.bfloat16)
        z_copies[c].append(
            (i, remote(terms[c].at[x, to_z], from_z[c].at[i], {"occ": occ, "vir": to_z * nx + x}))
        )

    outgoing = []

    def hand_over(first, values):
        at = pl.ds(first, WIDTH)
        out[:, at, :] = values.astype(jnp.bfloat16)
        outgoing.append(local(out.at[:, at, :], out_at.at[:, at, :]))

    def finish(c):
        total = x_total(c, nz - 1, z)
        for e, copy in z_copies[c]:
            copy.wait_recv()
            total += from_z[c][e].astype(jnp.float32)
        if not halves[c]:
            hand_over(c * WIDTH, total)
            return
        total = total.reshape(slots, HALF, 128)
        if (c - n_full) % 2 == 0:
            first_half[...] = total
            return
        both = jnp.concatenate([first_half[...], total], axis=1)
        first = (n_full + (c - n_full) // 2) * WIDTH
        hand_over(first, both)

    for what, c, *i in events_of(n_full, n_chunks, nz):
        if what == "gather":
            gather(c)
        elif what == "compute":
            compute(c)
        elif what == "own":
            compute_own(c)
        elif what == "pass":
            pass_on(c, *i)
        else:
            finish(c)
    for copy in outgoing:
        copy.wait()
    for copy in sent:
        copy.wait_send()


def body(nx, amplitudes, amp_slots, integrals, int_columns, slot_tile):
    _, slots, tile, _ = amplitudes.shape
    nv, no = lax.axis_size("vir"), lax.axis_size("occ")
    ny, nz = no // CORES, nv // nx
    owned, share = integrals.shape[:2]
    tiles = owned * share
    per_owner = slots // nv
    n_chunks = tile // WIDTH
    halves = (False,) * n_chunks
    if share % 2 == 0 and slots % 2 == 0:
        halves = halves[SPLIT:] + (True, True) * SPLIT
        n_chunks += SPLIT
    dims = (ny, nz, nx, slots, owned, share)

    ints = integrals.reshape(tiles, tile, tile)
    amps = amplitudes.reshape(nv, per_owner, tile, tile)

    bf16 = jnp.bfloat16
    held = [(no * tiles // 2, slots // 2) if half else (no * tiles, slots) for half in halves]
    scratch = [pltpu.VMEM((count + 1, WIDTH, tile), bf16) for count, _ in held]
    scratch += [pltpu.VMEM((nx, nz, part, WIDTH, tile), bf16) for _, part in held]
    scratch += [pltpu.VMEM((nx - 1, nz, part, WIDTH, tile), bf16) for _, part in held]
    scratch += [pltpu.VMEM((nz - 1, part, WIDTH, tile), bf16) for _, part in held]
    n_copies = copies_of(dims, n_chunks)
    scratch += [
        pltpu.VMEM((min(4, owned) * share, tile, tile), bf16),
        pltpu.VMEM(int_columns.shape, jnp.int32),
        pltpu.VMEM((nv, slots, 128), jnp.int32),
        pltpu.VMEM((nv, per_owner, tile, tile), bf16),
        pltpu.VMEM((nv, per_owner * tile, tile), bf16),
        pltpu.VMEM((nv, slots, 128), jnp.int32),
        pltpu.SMEM((nv, slots, 128), jnp.int32),
        pltpu.VMEM((slots, HALF, tile), jnp.float32),
        pltpu.SMEM(amp_slots.shape, jnp.int32),
        pltpu.SMEM(slot_tile.shape, jnp.int32),
        pltpu.VMEM(int_columns.shape[::-1], jnp.int32),
        pltpu.VMEM((slots, tile, tile), bf16),
        pltpu.SemaphoreType.REGULAR((nz - 1,)),
        pltpu.SemaphoreType.DMA((n_copies,)),
        pltpu.SemaphoreType.DMA((n_copies,)),
        pltpu.SemaphoreType.DMA((owned + 4 + nv + tile // WIDTH,)),
    ]
    result = pl.pallas_call(
        functools.partial(kernel, dims, halves),
        out_shape=jax.ShapeDtypeStruct((slots, tile, tile), bf16),
        in_specs=[
            pl.BlockSpec(memory_space=pl.ANY),
            pl.BlockSpec(memory_space=pl.ANY),
            pl.BlockSpec(memory_space=pl.ANY),
            pl.BlockSpec(memory_space=pl.ANY),
            pl.BlockSpec(memory_space=pl.ANY),
        ],
        out_specs=pl.BlockSpec(memory_space=pl.ANY),
        scratch_shapes=scratch,
        compiler_params=pltpu.CompilerParams(
            collective_id=0, has_side_effects=True, vmem_limit_bytes=66_000_000
        ),
    )(amp_slots, slot_tile, int_columns.T, amps, ints)
    return jnp.swapaxes(result, 1, 2)[None]


def solution(mesh):
    nv = mesh.shape["vir"]
    nx = nv // min(4, nv)
    in_specs = (
        P(("occ", "vir"), None, None, None),
        P(("occ", "vir"), None),
        P("vir", "occ", None, None),
        P(),
        P(),
    )
    out_specs = P(("occ", "vir"), None, None, None)
    return jax.shard_map(
        functools.partial(body, nx), mesh=mesh, in_specs=in_specs, out_specs=out_specs,
        check_vma=False,
    )
```

```python
import functools

import jax
import jax.numpy as jnp
from jax import lax
from jax.experimental import pallas as pl
from jax.experimental.pallas import tpu as pltpu
from jax.sharding import PartitionSpec as P

MESH = pl.DeviceIdType.MESH
CORES = 2
WIDTH = 16
HALF = 8
SPLIT = 2


def events_of(n_full, n_chunks, nz):
    events = []
    steps = list(range(nz - 1))

    def order(c):
        return [2, 0, 1] if c == 0 and nz == 4 else steps

    def passes(c, at):
        return [("pass", c, i) for i in at]

    for c in range(n_chunks):
        events.append(("gather", c))
        before, after = [], []
        if 0 < c < n_full:
            before = passes(c - 1, order(c - 1)[-1:])
        elif c >= n_full and c > 0:
            early = 0 if c == n_full + 1 else 1
            before = passes(c - 1, order(c - 1)[:early])
            after = passes(c - 1, order(c - 1)[early:])
        if c < n_full - 1 or c == n_full - 1 == n_chunks - 1:
            after += passes(c, order(c)[:-1])
        if 1 < c < n_full:
            after = [("finish", c - 2)] + after
        elif c > n_full and c > 2:
            after.append(("finish", c - 3))
        compute = [("compute", c), ("own", c)]
        if c == n_chunks - 1:
            after[2:2] = compute[1:]
            compute = compute[:1]
        events += before + compute + after
    listed = set(events)
    ends = [e for e in passes(n_chunks - 1, steps) if e not in listed]
    left = [("finish", c) for c in range(n_chunks) if ("finish", c) not in listed]
    return events + left[:-2] + ends + left[-2:]


def pieces_of(number, n_chunks, owned):
    if number == 0:
        return owned
    return 1


def copies_of(dims, n_chunks):
    ny, nz, nx, _, owned, _ = dims
    nv = nz * nx
    per_chunk = 1 + (nx - 1) * nz + (nz - 1)
    pieces = sum(pieces_of(number, n_chunks, owned) for number in range(n_chunks))
    return n_chunks * per_chunk + 2 * pieces * (ny - 1) + 2 * (nv - 1)


def kernel(dims, halves, slots_in, tiles_in, columns_in, amps_in, ints, out_at, *scratch):
    ny, nz, nx, slots, owned, share = dims
    n_chunks, n_full = len(halves), halves.count(False)
    tiles = owned * share
    nv, no = nz * nx, ny * CORES
    per_owner = slots // nv
    weights = scratch[:n_chunks]
    terms = scratch[n_chunks : 2 * n_chunks]
    from_x = scratch[2 * n_chunks : 3 * n_chunks]
    from_z = scratch[3 * n_chunks : 4 * n_chunks]
    (
        raw_ints, columns_of, tables, amp_raw, amps, tab_buf, tab_smem, first_half,
        own_slots, slot_tile, columns_t, out,
        near, send_sem, recv_sem, loc_sem,
    ) = scratch[4 * n_chunks :]

    occ, vir = lax.axis_index("occ"), lax.axis_index("vir")
    y, core = occ // CORES, lax.rem(occ, CORES)
    z, x = vir // nx, lax.rem(vir, nx)
    partner = y * CORES + (1 - core)

    def occ_at(step):
        return lax.rem(y + step, ny) * CORES + core

    def x_at(step):
        return lax.rem(x + step, nx)

    if nz == 4:
        z_to = [lax.rem(z + 2, 4), 3 - z, z + 1 - 2 * lax.rem(z, 2)]
        z_from = z_to
        inner = (z == 1) | (z == 2)
        hops = [[(2, None)], [(1, inner), (3, jnp.logical_not(inner))], [(1, None)]]
        near_first = [3, 2, 0, 1]
    else:
        z_to = [lax.rem(z + d, nz) for d in range(1, nz)]
        z_from = [lax.rem(z + nz - d, nz) for d in range(1, nz)]
        hops = [[(nz - 1, None)]] * (nz - 1)
        near_first = [nz - 1] + list(range(nz - 1))
    z_all, z_all_from = z_to + [z], z_from + [z]
    hops.append([(0, None)])

    counts = {"remote": 0, "local": 0}
    sent = []

    def planned(src, dst, where):
        at = counts["remote"]
        counts["remote"] += 1
        copy = pltpu.make_async_remote_copy(
            src_ref=src, dst_ref=dst, send_sem=send_sem.at[at], recv_sem=recv_sem.at[at],
            device_id=where, device_id_type=MESH,
        )
        sent.append(copy)
        return copy

    def remote(src, dst, where):
        copy = planned(src, dst, where)
        copy.start()
        return copy

    def local(src, dst):
        at = counts["local"]
        counts["local"] += 1
        copy = pltpu.make_async_copy(src, dst, loc_sem.at[at])
        copy.start()
        return copy

    def signal(sem, where):
        pl.semaphore_signal(sem, inc=1, device_id=where, device_id_type=MESH)

    def signal_plane(sem):
        for d in range(1, nx):
            signal(sem, {"occ": occ, "vir": z * nx + x_at(d)})

        @pl.when(z > 0)
        def _():
            signal(sem, {"occ": occ, "vir": vir - nx})

        @pl.when(z < nz - 1)
        def _():
            signal(sem, {"occ": occ, "vir": vir + nx})

    in_plane = (nx - 1) + (z + nz - 1) // nz + (2 * nz - 2 - z) // nz

    barrier = pltpu.get_barrier_semaphore()
    for d in range(1, ny):
        signal(barrier, {"occ": occ_at(d), "vir": vir})
    signal(barrier, {"occ": partner, "vir": vir})
    signal_plane(barrier)

    held = raw_ints.shape[0] // share

    def fetch(g):
        return local(
            ints.at[pl.ds(g * share, share)], raw_ints.at[pl.ds((g % held) * share, share)]
        )

    pieces_in = [fetch(g) for g in range(held)]
    amp_own = local(amps_in.at[vir], amp_raw.at[vir])
    lists_in = [
        local(slots_in, own_slots), local(tiles_in, slot_tile), local(columns_in, columns_t),
    ]

    def span(number, source, piece=0, pieces=1):
        held_tiles = tiles // 2 if halves[number] else tiles
        count = held_tiles // pieces
        return weights[number].at[pl.ds(source * held_tiles + piece * count, count)]

    for number in range(n_chunks):
        spare = no * tiles // 2 if halves[number] else no * tiles
        weights[number][spare] = jnp.zeros((WIDTH, 128), jnp.bfloat16)

    pair = 2 if n_full < n_chunks else 1

    def turn(slot, tile):
        turned = [raw_ints[slot + e].T for e in range(pair)]
        for e in range(pair):
            for number in range(n_full):
                weights[number][occ * tiles + tile + e] = turned[e][number * WIDTH : (number + 1) * WIDTH]
        for number in range(n_full, n_chunks, 2):
            first = (n_full + (number - n_full) // 2) * WIDTH
            tails = [one[first : first + WIDTH].astype(jnp.float32) for one in turned]
            for h in range(2):
                both = jnp.concatenate([tail[h * HALF : (h + 1) * HALF] for tail in tails], axis=0)
                weights[number + h][(occ * tiles + tile) // 2] = both.astype(jnp.bfloat16)

    across = {number: [[] for _ in range(ny - 1)] for number in range(n_chunks)}

    def start_lead(g):
        piece = span(0, occ, g, owned)
        for d in range(1, ny):
            across[0][d - 1].append(remote(piece, piece, {"occ": occ_at(d), "vir": vir}))

    def start_across(number):
        pieces = pieces_of(number, n_chunks, owned)
        for p in range(pieces):
            piece = span(number, occ, p, pieces)
            for d in range(1, ny):
                across[number][d - 1].append(
                    remote(piece, piece, {"occ": occ_at(d), "vir": vir})
                )

    amp_copies = {}
    for i in range(nz):
        for d in range(1 if i == nz - 1 else 0, nx):
            to = z_all[i] * nx + x_at(d)
            amp_copies[i, d] = planned(
                amps_in.at[to], amp_raw.at[vir], {"occ": occ, "vir": to}
            )

    def send_amps(level):
        for (i, d), copy in amp_copies.items():
            for hop, when in hops[i]:
                if hop + (1 if d else 0) == level:
                    if when is None:
                        copy.start()
                    else:
                        pl.when(when)(copy.start)

    lanes = lax.broadcasted_iota(jnp.int32, (slots, 128), 1)

    def make_table(v, wanted, place):
        mapped = jnp.zeros((slots, 128), jnp.int32)
        for k in range(per_owner):
            mine = own_slots[0, v * per_owner + k]
            reached = columns_of[pl.ds(v * owned + mine, 1), :]
            found = jnp.where(reached == wanted, place + mine * share, no * tiles)
            mapped = jnp.where(lanes == k, jnp.min(found, axis=1, keepdims=True), mapped)
        tables[v] = mapped

    relays = [1 + level * max(1, (owned - 2) // (nz - 1)) for level in range(nz)]
    tab_copies = {}
    for g in range(owned):
        pieces_in[g].wait()

        @pl.loop(0, share // pair)
        def _(j, g=g):
            turn((g % held) * share + pair * j, g * share + pair * j)

        if g + held < owned:
            pieces_in.append(fetch(g + held))

        if g == 0:
            pl.semaphore_wait(barrier, ny + in_plane)
        start_lead(g)
        if g == 0:
            send_amps(1)
            for copy in lists_in:
                copy.wait()
            columns_of[...] = columns_t[...].T
            rows = lax.broadcasted_iota(jnp.int32, (slots, share * no), 0)
            entry = lax.broadcasted_iota(jnp.int32, (slots, share * no), 1)
            place = (entry // share) * tiles + lax.rem(entry, share)
            wanted = jnp.zeros((slots, share * no), jnp.int32)
            for s in range(slots):
                wanted = jnp.where(rows == s, slot_tile[(s // per_owner) * owned + own_slots[0, s]], wanted)
        if g in relays:
            level = relays.index(g)
            if level > 0:
                pl.semaphore_wait(near.at[level - 1], in_plane)
                send_amps(level + 1)
            if level < nz - 1:
                signal_plane(near.at[level])
        for v in range(g * nv // owned, (g + 1) * nv // owned):
            make_table(v, wanted, place)
        if g == owned - 1:
            tab_own = local(tables.at[vir], tab_smem.at[vir])
            for i in near_first:
                for d in range(1 if i == nz - 1 else 0, nx):
                    to = z_all[i] * nx + x_at(d)
                    tab_copies[i, d] = remote(
                        tables.at[to], tab_buf.at[vir], {"occ": occ, "vir": to}
                    )

    for number in range(1, n_chunks):
        start_across(number)

    side = {}
    for number in range(n_chunks):
        side[number] = [
            remote(span(number, occ), span(number, occ), {"occ": partner, "vir": vir})
        ]

    def turn_amps(v):
        for k in range(per_owner):
            amps[v, k * 128 : (k + 1) * 128, :] = amp_raw[v, k].T

    amp_own.wait()
    tab_own.wait()
    turn_amps(vir)

    def prepare(i):
        started = []
        for d in range(1 if i == nz - 1 else 0, nx):
            source = z_all_from[i] * nx + lax.rem(x + nx - d, nx)
            tab_copies[i, d].wait_recv()
            started.append(local(tab_buf.at[source], tab_smem.at[source]))
        for d in range(1 if i == nz - 1 else 0, nx):
            source = z_all_from[i] * nx + lax.rem(x + nx - d, nx)
            amp_copies[i, d].wait_recv()
            turn_amps(source)
        for copy in started:
            copy.wait()

    if nz != 4:
        for i in near_first:
            prepare(i)

    x_copies = {c: [[] for _ in range(nz)] for c in range(n_chunks)}
    z_copies = {c: [] for c in range(n_chunks)}

    def gather(c):
        for d in range(1, ny):
            source = lax.rem(y - d + ny, ny) * CORES + core
            for p, copy in enumerate(across[c][d - 1]):
                copy.wait_recv()
                piece = span(c, source, p, len(across[c][d - 1]))
                side[c].append(remote(piece, piece, {"occ": partner, "vir": vir}))

    def product(c, to_x, to_z):
        r = to_z * nx + to_x
        if halves[c]:
            half_product(c, r, to_x, to_z)
            return
        columns = []
        for k in range(per_owner):
            pieces = [weights[c][tab_smem[r, s, k]] for s in range(slots)]
            columns.append(jnp.concatenate(pieces, axis=0))
        left = jnp.concatenate(columns, axis=1)
        prod = jnp.dot(left, amps[r], preferred_element_type=jnp.float32)
        terms[c][to_x, to_z] = prod.astype(jnp.bfloat16).reshape(slots, WIDTH, 128)

    def half_product(c, r, to_x, to_z):
        total = None
        for k in range(per_owner):
            at = [tab_smem[r, s, k] for s in range(slots)]
            left = jnp.concatenate(
                [weights[c][lax.shift_right_logical(a, 1)] for a in at], axis=0
            )
            prod = jnp.dot(
                left, amps[r, k * 128 : (k + 1) * 128, :], preferred_element_type=jnp.float32
            )
            picked = []
            for s, a in enumerate(at):
                low = prod[s * WIDTH : s * WIDTH + HALF]
                high = prod[s * WIDTH + HALF : (s + 1) * WIDTH]
                picked.append(jnp.where(lax.bitwise_and(a, 1) == 1, high, low))
            picked = jnp.concatenate(picked, axis=0)
            total = picked if total is None else total + picked
        terms[c][to_x, to_z] = total.reshape(slots // 2, WIDTH, 128).astype(jnp.bfloat16)

    def compute(c):
        for copy in side[c]:
            copy.wait_recv()
        for i in near_first if c == 0 else range(nz):
            to_z = z_all[i]
            if c == 0 and nz == 4:
                prepare(i)
            for d in range(1, nx):
                to_x = x_at(d)
                product(c, to_x, to_z)
                x_copies[c][i].append(
                    remote(
                        terms[c].at[to_x, to_z], from_x[c].at[d - 1, to_z],
                        {"occ": occ, "vir": z * nx + to_x},
                    )
                )

    def compute_own(c):
        for to_z in z_all:
            product(c, x, to_z)

    def x_total(c, i, to_z):
        for copy in x_copies[c][i]:
            copy.wait_recv()
        total = terms[c][x, to_z].astype(jnp.float32)
        for e in range(nx - 1):
            total += from_x[c][e, to_z].astype(jnp.float32)
        return total

    def pass_on(c, i):
        to_z = z_to[i]
        terms[c][x, to_z] = x_total(c, i, to_z).astype(jnp.bfloat16)
        z_copies[c].append(
            (i, remote(terms[c].at[x, to_z], from_z[c].at[i], {"occ": occ, "vir": to_z * nx + x}))
        )

    outgoing = []

    def hand_over(first, values):
        at = pl.ds(first, WIDTH)
        out[:, at, :] = values.astype(jnp.bfloat16)
        outgoing.append(local(out.at[:, at, :], out_at.at[:, at, :]))

    def finish(c):
        total = x_total(c, nz - 1, z)
        for e, copy in z_copies[c]:
            copy.wait_recv()
            total += from_z[c][e].astype(jnp.float32)
        if not halves[c]:
            hand_over(c * WIDTH, total)
            return
        total = total.reshape(slots, HALF, 128)
        if (c - n_full) % 2 == 0:
            first_half[...] = total
            return
        both = jnp.concatenate([first_half[...], total], axis=1)
        first = (n_full + (c - n_full) // 2) * WIDTH
        hand_over(first, both)

    for what, c, *i in events_of(n_full, n_chunks, nz):
        if what == "gather":
            gather(c)
        elif what == "compute":
            compute(c)
        elif what == "own":
            compute_own(c)
        elif what == "pass":
            pass_on(c, *i)
        else:
            finish(c)
    for copy in outgoing:
        copy.wait()
    for copy in sent:
        copy.wait_send()


def body(nx, amplitudes, amp_slots, integrals, int_columns, slot_tile):
    _, slots, tile, _ = amplitudes.shape
    nv, no = lax.axis_size("vir"), lax.axis_size("occ")
    ny, nz = no // CORES, nv // nx
    owned, share = integrals.shape[:2]
    tiles = owned * share
    per_owner = slots // nv
    n_chunks = tile // WIDTH
    halves = (False,) * n_chunks
    if share % 2 == 0 and slots % 2 == 0:
        halves = halves[SPLIT:] + (True, True) * SPLIT
        n_chunks += SPLIT
    dims = (ny, nz, nx, slots, owned, share)

    ints = integrals.reshape(tiles, tile, tile)
    amps = amplitudes.reshape(nv, per_owner, tile, tile)

    bf16 = jnp.bfloat16
    held = [(no * tiles // 2, slots // 2) if half else (no * tiles, slots) for half in halves]
    scratch = [pltpu.VMEM((count + 1, WIDTH, tile), bf16) for count, _ in held]
    scratch += [pltpu.VMEM((nx, nz, part, WIDTH, tile), bf16) for _, part in held]
    scratch += [pltpu.VMEM((nx - 1, nz, part, WIDTH, tile), bf16) for _, part in held]
    scratch += [pltpu.VMEM((nz - 1, part, WIDTH, tile), bf16) for _, part in held]
    n_copies = copies_of(dims, n_chunks)
    scratch += [
        pltpu.VMEM((min(4, owned) * share, tile, tile), bf16),
        pltpu.VMEM(int_columns.shape, jnp.int32),
        pltpu.VMEM((nv, slots, 128), jnp.int32),
        pltpu.VMEM((nv, per_owner, tile, tile), bf16),
        pltpu.VMEM((nv, per_owner * tile, tile), bf16),
        pltpu.VMEM((nv, slots, 128), jnp.int32),
        pltpu.SMEM((nv, slots, 128), jnp.int32),
        pltpu.VMEM((slots, HALF, tile), jnp.float32),
        pltpu.SMEM(amp_slots.shape, jnp.int32),
        pltpu.SMEM(slot_tile.shape, jnp.int32),
        pltpu.VMEM(int_columns.shape[::-1], jnp.int32),
        pltpu.VMEM((slots, tile, tile), bf16),
        pltpu.SemaphoreType.REGULAR((nz - 1,)),
        pltpu.SemaphoreType.DMA((n_copies,)),
        pltpu.SemaphoreType.DMA((n_copies,)),
        pltpu.SemaphoreType.DMA((owned + 4 + nv + tile // WIDTH,)),
    ]
    result = pl.pallas_call(
        functools.partial(kernel, dims, halves),
        out_shape=jax.ShapeDtypeStruct((slots, tile, tile), bf16),
        in_specs=[
            pl.BlockSpec(memory_space=pl.ANY),
            pl.BlockSpec(memory_space=pl.ANY),
            pl.BlockSpec(memory_space=pl.ANY),
            pl.BlockSpec(memory_space=pl.ANY),
            pl.BlockSpec(memory_space=pl.ANY),
        ],
        out_specs=pl.BlockSpec(memory_space=pl.ANY),
        scratch_shapes=scratch,
        compiler_params=pltpu.CompilerParams(
            collective_id=0, has_side_effects=True, vmem_limit_bytes=66_000_000
        ),
    )(amp_slots, slot_tile, int_columns.T, amps, ints)
    return jnp.swapaxes(result, 1, 2)[None]


def solution(mesh):
    nv = mesh.shape["vir"]
    nx = nv // min(4, nv)
    in_specs = (
        P(("occ", "vir"), None, None, None),
        P(("occ", "vir"), None),
        P("vir", "occ", None, None),
        P(),
        P(),
    )
    out_specs = P(("occ", "vir"), None, None, None)
    return jax.shard_map(
        functools.partial(body, nx), mesh=mesh, in_specs=in_specs, out_specs=out_specs,
        check_vma=False,
    )
```

```python
import functools

import jax
import jax.numpy as jnp
from jax import lax
from jax.experimental import pallas as pl
from jax.experimental.pallas import tpu as pltpu
from jax.sharding import PartitionSpec as P

MESH = pl.DeviceIdType.MESH
CORES = 2
WIDTH = 16
HALF = 8
SPLIT = 3


def events_of(n_full, n_chunks, nz):
    events = []
    steps = list(range(nz - 1))

    def order(c):
        return [2, 0, 1] if c == 0 and nz == 4 else steps

    def passes(c, at):
        return [("pass", c, i) for i in at]

    for c in range(n_chunks):
        events.append(("gather", c))
        before, after = [], []
        if 0 < c < n_full:
            before = passes(c - 1, order(c - 1)[-1:])
        elif c >= n_full and c > 0:
            early = 0 if c == n_full + 1 else 1
            before = passes(c - 1, order(c - 1)[:early])
            after = passes(c - 1, order(c - 1)[early:])
        if c < n_full - 1 or c == n_full - 1 == n_chunks - 1:
            after += passes(c, order(c)[:-1])
        if 1 < c < n_full:
            after = [("finish", c - 2)] + after
        elif c > n_full and c > 2:
            after.append(("finish", c - 3))
        compute = [("compute", c), ("own", c)]
        if c == n_chunks - 1:
            after[2:2] = compute[1:]
            compute = compute[:1]
        events += before + compute + after
    listed = set(events)
    ends = [e for e in passes(n_chunks - 1, steps) if e not in listed]
    left = [("finish", c) for c in range(n_chunks) if ("finish", c) not in listed]
    return events + left[:-2] + ends + left[-2:]


def pieces_of(number, n_chunks, owned):
    if number == 0:
        return owned
    return 1


def copies_of(dims, n_chunks):
    ny, nz, nx, _, owned, _ = dims
    nv = nz * nx
    per_chunk = 1 + (nx - 1) * nz + (nz - 1)
    pieces = sum(pieces_of(number, n_chunks, owned) for number in range(n_chunks))
    return n_chunks * per_chunk + 2 * pieces * (ny - 1) + 2 * (nv - 1)


def kernel(dims, halves, slots_in, tiles_in, columns_in, amps_in, ints, out_at, *scratch):
    ny, nz, nx, slots, owned, share = dims
    n_chunks, n_full = len(halves), halves.count(False)
    tiles = owned * share
    nv, no = nz * nx, ny * CORES
    per_owner = slots // nv
    weights = scratch[:n_chunks]
    terms = scratch[n_chunks : 2 * n_chunks]
    from_x = scratch[2 * n_chunks : 3 * n_chunks]
    from_z = scratch[3 * n_chunks : 4 * n_chunks]
    (
        raw_ints, columns_of, tables, amp_raw, amps, tab_buf, tab_smem, first_half,
        own_slots, slot_tile, columns_t, out,
        near, send_sem, recv_sem, loc_sem,
    ) = scratch[4 * n_chunks :]

    occ, vir = lax.axis_index("occ"), lax.axis_index("vir")
    y, core = occ // CORES, lax.rem(occ, CORES)
    z, x = vir // nx, lax.rem(vir, nx)
    partner = y * CORES + (1 - core)

    def occ_at(step):
        return lax.rem(y + step, ny) * CORES + core

    def x_at(step):
        return lax.rem(x + step, nx)

    if nz == 4:
        z_to = [lax.rem(z + 2, 4), 3 - z, z + 1 - 2 * lax.rem(z, 2)]
        z_from = z_to
        inner = (z == 1) | (z == 2)
        hops = [[(2, None)], [(1, inner), (3, jnp.logical_not(inner))], [(1, None)]]
        near_first = [3, 2, 0, 1]
    else:
        z_to = [lax.rem(z + d, nz) for d in range(1, nz)]
        z_from = [lax.rem(z + nz - d, nz) for d in range(1, nz)]
        hops = [[(nz - 1, None)]] * (nz - 1)
        near_first = [nz - 1] + list(range(nz - 1))
    z_all, z_all_from = z_to + [z], z_from + [z]
    hops.append([(0, None)])

    counts = {"remote": 0, "local": 0}
    sent = []

    def planned(src, dst, where):
        at = counts["remote"]
        counts["remote"] += 1
        copy = pltpu.make_async_remote_copy(
            src_ref=src, dst_ref=dst, send_sem=send_sem.at[at], recv_sem=recv_sem.at[at],
            device_id=where, device_id_type=MESH,
        )
        sent.append(copy)
        return copy

    def remote(src, dst, where):
        copy = planned(src, dst, where)
        copy.start()
        return copy

    def local(src, dst):
        at = counts["local"]
        counts["local"] += 1
        copy = pltpu.make_async_copy(src, dst, loc_sem.at[at])
        copy.start()
        return copy

    def signal(sem, where):
        pl.semaphore_signal(sem, inc=1, device_id=where, device_id_type=MESH)

    def signal_plane(sem):
        for d in range(1, nx):
            signal(sem, {"occ": occ, "vir": z * nx + x_at(d)})

        @pl.when(z > 0)
        def _():
            signal(sem, {"occ": occ, "vir": vir - nx})

        @pl.when(z < nz - 1)
        def _():
            signal(sem, {"occ": occ, "vir": vir + nx})

    in_plane = (nx - 1) + (z + nz - 1) // nz + (2 * nz - 2 - z) // nz

    barrier = pltpu.get_barrier_semaphore()
    for d in range(1, ny):
        signal(barrier, {"occ": occ_at(d), "vir": vir})
    signal(barrier, {"occ": partner, "vir": vir})
    signal_plane(barrier)

    held = raw_ints.shape[0] // share

    def fetch(g):
        return local(
            ints.at[pl.ds(g * share, share)], raw_ints.at[pl.ds((g % held) * share, share)]
        )

    pieces_in = [fetch(g) for g in range(held)]
    amp_own = local(amps_in.at[vir], amp_raw.at[vir])
    lists_in = [
        local(slots_in, own_slots), local(tiles_in, slot_tile), local(columns_in, columns_t),
    ]

    def span(number, source, piece=0, pieces=1):
        held_tiles = tiles // 2 if halves[number] else tiles
        count = held_tiles // pieces
        return weights[number].at[pl.ds(source * held_tiles + piece * count, count)]

    for number in range(n_chunks):
        spare = no * tiles // 2 if halves[number] else no * tiles
        weights[number][spare] = jnp.zeros((WIDTH, 128), jnp.bfloat16)

    pair = 2 if n_full < n_chunks else 1

    def turn(slot, tile):
        turned = [raw_ints[slot + e].T for e in range(pair)]
        for e in range(pair):
            for number in range(n_full):
                weights[number][occ * tiles + tile + e] = turned[e][number * WIDTH : (number + 1) * WIDTH]
        for number in range(n_full, n_chunks, 2):
            first = (n_full + (number - n_full) // 2) * WIDTH
            tails = [one[first : first + WIDTH].astype(jnp.float32) for one in turned]
            for h in range(2):
                both = jnp.concatenate([tail[h * HALF : (h + 1) * HALF] for tail in tails], axis=0)
                weights[number + h][(occ * tiles + tile) // 2] = both.astype(jnp.bfloat16)

    across = {number: [[] for _ in range(ny - 1)] for number in range(n_chunks)}

    def start_lead(g):
        piece = span(0, occ, g, owned)
        for d in range(1, ny):
            across[0][d - 1].append(remote(piece, piece, {"occ": occ_at(d), "vir": vir}))

    def start_across(number):
        pieces = pieces_of(number, n_chunks, owned)
        for p in range(pieces):
            piece = span(number, occ, p, pieces)
            for d in range(1, ny):
                across[number][d - 1].append(
                    remote(piece, piece, {"occ": occ_at(d), "vir": vir})
                )

    amp_copies = {}
    for i in range(nz):
        for d in range(1 if i == nz - 1 else 0, nx):
            to = z_all[i] * nx + x_at(d)
            amp_copies[i, d] = planned(
                amps_in.at[to], amp_raw.at[vir], {"occ": occ, "vir": to}
            )

    def send_amps(level):
        for (i, d), copy in amp_copies.items():
            for hop, when in hops[i]:
                if hop + (1 if d else 0) == level:
                    if when is None:
                        copy.start()
                    else:
                        pl.when(when)(copy.start)

    lanes = lax.broadcasted_iota(jnp.int32, (slots, 128), 1)

    def make_table(v, wanted, place):
        mapped = jnp.zeros((slots, 128), jnp.int32)
        for k in range(per_owner):
            mine = own_slots[0, v * per_owner + k]
            reached = columns_of[pl.ds(v * owned + mine, 1), :]
            found = jnp.where(reached == wanted, place + mine * share, no * tiles)
            mapped = jnp.where(lanes == k, jnp.min(found, axis=1, keepdims=True), mapped)
        tables[v] = mapped

    relays = [1 + level * max(1, (owned - 2) // (nz - 1)) for level in range(nz)]
    tab_copies = {}
    for g in range(owned):
        pieces_in[g].wait()

        @pl.loop(0, share // pair)
        def _(j, g=g):
            turn((g % held) * share + pair * j, g * share + pair * j)

        if g + held < owned:
            pieces_in.append(fetch(g + held))

        if g == 0:
            pl.semaphore_wait(barrier, ny + in_plane)
        start_lead(g)
        if g == 0:
            send_amps(1)
            for copy in lists_in:
                copy.wait()
            columns_of[...] = columns_t[...].T
            rows = lax.broadcasted_iota(jnp.int32, (slots, share * no), 0)
            entry = lax.broadcasted_iota(jnp.int32, (slots, share * no), 1)
            place = (entry // share) * tiles + lax.rem(entry, share)
            wanted = jnp.zeros((slots, share * no), jnp.int32)
            for s in range(slots):
                wanted = jnp.where(rows == s, slot_tile[(s // per_owner) * owned + own_slots[0, s]], wanted)
        if g in relays:
            level = relays.index(g)
            if level > 0:
                pl.semaphore_wait(near.at[level - 1], in_plane)
                send_amps(level + 1)
            if level < nz - 1:
                signal_plane(near.at[level])
        for v in range(g * nv // owned, (g + 1) * nv // owned):
            make_table(v, wanted, place)
        if g == owned - 1:
            tab_own = local(tables.at[vir], tab_smem.at[vir])
            for i in near_first:
                for d in range(1 if i == nz - 1 else 0, nx):
                    to = z_all[i] * nx + x_at(d)
                    tab_copies[i, d] = remote(
                        tables.at[to], tab_buf.at[vir], {"occ": occ, "vir": to}
                    )

    for number in range(1, n_chunks):
        start_across(number)

    side = {}
    for number in range(n_chunks):
        side[number] = [
            remote(span(number, occ), span(number, occ), {"occ": partner, "vir": vir})
        ]

    def turn_amps(v):
        for k in range(per_owner):
            amps[v, k * 128 : (k + 1) * 128, :] = amp_raw[v, k].T

    amp_own.wait()
    tab_own.wait()
    turn_amps(vir)

    def prepare(i):
        started = []
        for d in range(1 if i == nz - 1 else 0, nx):
            source = z_all_from[i] * nx + lax.rem(x + nx - d, nx)
            tab_copies[i, d].wait_recv()
            started.append(local(tab_buf.at[source], tab_smem.at[source]))
        for d in range(1 if i == nz - 1 else 0, nx):
            source = z_all_from[i] * nx + lax.rem(x + nx - d, nx)
            amp_copies[i, d].wait_recv()
            turn_amps(source)
        for copy in started:
            copy.wait()

    if nz != 4:
        for i in near_first:
            prepare(i)

    x_copies = {c: [[] for _ in range(nz)] for c in range(n_chunks)}
    z_copies = {c: [] for c in range(n_chunks)}

    def gather(c):
        for d in range(1, ny):
            source = lax.rem(y - d + ny, ny) * CORES + core
            for p, copy in enumerate(across[c][d - 1]):
                copy.wait_recv()
                piece = span(c, source, p, len(across[c][d - 1]))
                side[c].append(remote(piece, piece, {"occ": partner, "vir": vir}))

    def product(c, to_x, to_z):
        r = to_z * nx + to_x
        if halves[c]:
            half_product(c, r, to_x, to_z)
            return
        columns = []
        for k in range(per_owner):
            pieces = [weights[c][tab_smem[r, s, k]] for s in range(slots)]
            columns.append(jnp.concatenate(pieces, axis=0))
        left = jnp.concatenate(columns, axis=1)
        prod = jnp.dot(left, amps[r], preferred_element_type=jnp.float32)
        terms[c][to_x, to_z] = prod.astype(jnp.bfloat16).reshape(slots, WIDTH, 128)

    def half_product(c, r, to_x, to_z):
        total = None
        for k in range(per_owner):
            at = [tab_smem[r, s, k] for s in range(slots)]
            left = jnp.concatenate(
                [weights[c][lax.shift_right_logical(a, 1)] for a in at], axis=0
            )
            prod = jnp.dot(
                left, amps[r, k * 128 : (k + 1) * 128, :], preferred_element_type=jnp.float32
            )
            picked = []
            for s, a in enumerate(at):
                low = prod[s * WIDTH : s * WIDTH + HALF]
                high = prod[s * WIDTH + HALF : (s + 1) * WIDTH]
                picked.append(jnp.where(lax.bitwise_and(a, 1) == 1, high, low))
            picked = jnp.concatenate(picked, axis=0)
            total = picked if total is None else total + picked
        terms[c][to_x, to_z] = total.reshape(slots // 2, WIDTH, 128).astype(jnp.bfloat16)

    def compute(c):
        for copy in side[c]:
            copy.wait_recv()
        for i in near_first if c == 0 else range(nz):
            to_z = z_all[i]
            if c == 0 and nz == 4:
                prepare(i)
            for d in range(1, nx):
                to_x = x_at(d)
                product(c, to_x, to_z)
                x_copies[c][i].append(
                    remote(
                        terms[c].at[to_x, to_z], from_x[c].at[d - 1, to_z],
                        {"occ": occ, "vir": z * nx + to_x},
                    )
                )

    def compute_own(c):
        for to_z in z_all:
            product(c, x, to_z)

    def x_total(c, i, to_z):
        for copy in x_copies[c][i]:
            copy.wait_recv()
        total = terms[c][x, to_z].astype(jnp.float32)
        for e in range(nx - 1):
            total += from_x[c][e, to_z].astype(jnp.float32)
        return total

    def pass_on(c, i):
        to_z = z_to[i]
        terms[c][x, to_z] = x_total(c, i, to_z).astype(jnp.bfloat16)
        z_copies[c].append(
            (i, remote(terms[c].at[x, to_z], from_z[c].at[i], {"occ": occ, "vir": to_z * nx + x}))
        )

    outgoing = []

    def hand_over(first, values):
        at = pl.ds(first, WIDTH)
        out[:, at, :] = values.astype(jnp.bfloat16)
        outgoing.append(local(out.at[:, at, :], out_at.at[:, at, :]))

    def finish(c):
        total = x_total(c, nz - 1, z)
        for e, copy in z_copies[c]:
            copy.wait_recv()
            total += from_z[c][e].astype(jnp.float32)
        if not halves[c]:
            hand_over(c * WIDTH, total)
            return
        total = total.reshape(slots, HALF, 128)
        if (c - n_full) % 2 == 0:
            first_half[...] = total
            return
        both = jnp.concatenate([first_half[...], total], axis=1)
        first = (n_full + (c - n_full) // 2) * WIDTH
        hand_over(first, both)

    for what, c, *i in events_of(n_full, n_chunks, nz):
        if what == "gather":
            gather(c)
        elif what == "compute":
            compute(c)
        elif what == "own":
            compute_own(c)
        elif what == "pass":
            pass_on(c, *i)
        else:
            finish(c)
    for copy in outgoing:
        copy.wait()
    for copy in sent:
        copy.wait_send()


def body(nx, amplitudes, amp_slots, integrals, int_columns, slot_tile):
    _, slots, tile, _ = amplitudes.shape
    nv, no = lax.axis_size("vir"), lax.axis_size("occ")
    ny, nz = no // CORES, nv // nx
    owned, share = integrals.shape[:2]
    tiles = owned * share
    per_owner = slots // nv
    n_chunks = tile // WIDTH
    halves = (False,) * n_chunks
    if share % 2 == 0 and slots % 2 == 0:
        halves = halves[SPLIT:] + (True, True) * SPLIT
        n_chunks += SPLIT
    dims = (ny, nz, nx, slots, owned, share)

    ints = integrals.reshape(tiles, tile, tile)
    amps = amplitudes.reshape(nv, per_owner, tile, tile)

    bf16 = jnp.bfloat16
    held = [(no * tiles // 2, slots // 2) if half else (no * tiles, slots) for half in halves]
    scratch = [pltpu.VMEM((count + 1, WIDTH, tile), bf16) for count, _ in held]
    scratch += [pltpu.VMEM((nx, nz, part, WIDTH, tile), bf16) for _, part in held]
    scratch += [pltpu.VMEM((nx - 1, nz, part, WIDTH, tile), bf16) for _, part in held]
    scratch += [pltpu.VMEM((nz - 1, part, WIDTH, tile), bf16) for _, part in held]
    n_copies = copies_of(dims, n_chunks)
    scratch += [
        pltpu.VMEM((min(4, owned) * share, tile, tile), bf16),
        pltpu.VMEM(int_columns.shape, jnp.int32),
        pltpu.VMEM((nv, slots, 128), jnp.int32),
        pltpu.VMEM((nv, per_owner, tile, tile), bf16),
        pltpu.VMEM((nv, per_owner * tile, tile), bf16),
        pltpu.VMEM((nv, slots, 128), jnp.int32),
        pltpu.SMEM((nv, slots, 128), jnp.int32),
        pltpu.VMEM((slots, HALF, tile), jnp.float32),
        pltpu.SMEM(amp_slots.shape, jnp.int32),
        pltpu.SMEM(slot_tile.shape, jnp.int32),
        pltpu.VMEM(int_columns.shape[::-1], jnp.int32),
        pltpu.VMEM((slots, tile, tile), bf16),
        pltpu.SemaphoreType.REGULAR((nz - 1,)),
        pltpu.SemaphoreType.DMA((n_copies,)),
        pltpu.SemaphoreType.DMA((n_copies,)),
        pltpu.SemaphoreType.DMA((owned + 4 + nv + tile // WIDTH,)),
    ]
    result = pl.pallas_call(
        functools.partial(kernel, dims, halves),
        out_shape=jax.ShapeDtypeStruct((slots, tile, tile), bf16),
        in_specs=[
            pl.BlockSpec(memory_space=pl.ANY),
            pl.BlockSpec(memory_space=pl.ANY),
            pl.BlockSpec(memory_space=pl.ANY),
            pl.BlockSpec(memory_space=pl.ANY),
            pl.BlockSpec(memory_space=pl.ANY),
        ],
        out_specs=pl.BlockSpec(memory_space=pl.ANY),
        scratch_shapes=scratch,
        compiler_params=pltpu.CompilerParams(
            collective_id=0, has_side_effects=True, vmem_limit_bytes=66_000_000
        ),
    )(amp_slots, slot_tile, int_columns.T, amps, ints)
    return jnp.swapaxes(result, 1, 2)[None]


def solution(mesh):
    nv = mesh.shape["vir"]
    nx = nv // min(4, nv)
    in_specs = (
        P(("occ", "vir"), None, None, None),
        P(("occ", "vir"), None),
        P("vir", "occ", None, None),
        P(),
        P(),
    )
    out_specs = P(("occ", "vir"), None, None, None)
    return jax.shard_map(
        functools.partial(body, nx), mesh=mesh, in_specs=in_specs, out_specs=out_specs,
        check_vma=False,
    )
```
